256 devices in a mesh: lat: 16 (over y, z_hi), lon: 8 (over z_lo, x), comp: 2 (over core).
Axes of the slice: x: 4, y: 4, z: 8 (z_hi: 4, z_lo: 2; z = z_hi * 2 + z_lo), core: 2. Of those that a mesh axis runs over, the one named last changes fastest.
Arguments:
- atm_state: bfloat16 [384, 1024, 384], P('lat', ('lon', 'comp')), may hold values from -6 to 6
- ocean_state: bfloat16 [384, 1024, 256], P(('lat', 'comp'), 'lon'), may hold values from -6 to 6
- wet_mask: int32 [384, 1024], P(('lat', 'comp'), 'lon'), may hold values 0 or 1
- legendre: bfloat16 [512, 384, 384], P(('lat', 'lon', 'comp')), may hold values from -4 to 4
- quad_weight: float32 [384], replicated, may hold values from 0.5 to 2
- spec_real: bfloat16 [384, 384], replicated, may hold values from -0.3125 to 0.3125
- spec_imag: bfloat16 [384, 384], replicated, may hold values from -0.3125 to 0.3125
- degree_gain: float32 [384], replicated, may hold values from 0.5 to 2
- atm_gain: float32 [2, 384], replicated, may hold values from 0.1 to 1.9
- atm_up: bfloat16 [384, 768], replicated, may hold values from -0.3125 to 0.3125
- atm_down: bfloat16 [768, 384], replicated, may hold values from -0.21875 to 0.21875
- atm_to_surface: bfloat16 [384, 32], replicated, may hold values from -0.3125 to 0.3125
- surface_to_atm: bfloat16 [32, 384], replicated, may hold values from -1 to 1
- ocean_to_surface: bfloat16 [256, 32], replicated, may hold values from -0.375 to 0.375
- surface_to_ocean: bfloat16 [32, 256], replicated, may hold values from -1 to 1
- ocean_kernel: bfloat16 [2, 7, 7, 256], replicated, may hold values from -0.875 to 0.875
- ocean_gain: float32 [2, 256], replicated, may hold values from 0.1 to 1.9
- ocean_up: bfloat16 [2, 256, 1024], replicated, may hold values from -0.375 to 0.375
- ocean_down: bfloat16 [2, 1024, 256], replicated, may hold values from -0.1875 to 0.1875
Outputs:
- atm_out: bfloat16 [384, 1024, 384], P('lat', ('lon', 'comp'))
- ocean_out: bfloat16 [384, 1024, 256], P(('lat', 'comp'), 'lon')
The draws below stay inside these ranges and needn't reach their ends.
All inputs are finite; a program needn't handle non-finite values. No bound on the sum of `wet_mask` on one device may be relied on, other than what follows from the above.
Results may differ from the reference program's by a relative error of at most 0.01.
Values may be sent and summed in bfloat16 or wider, within the bound.
No kernel may reach another device: no remote copies, remote signals or barrier semaphores. Data moves between devices by JAX's collectives and lax.ppermute only.
A program may use at most 128 MiB of HBM per device.

```python
import math
import jax
import jax.numpy as jnp
from jax import lax

C = 384
HID = 768
OC = 256
OHID = 1024
SURF = 32
MODES = 512
DEG = 384
STENCIL_TAPS = 7
OCEAN_DILATION = 2
LAT_DEV = 24
NLAT = 384
NLON = 1024
MODES_DEV = 2
N_LAT = 16
DEVICES = 256


def with_ends(entries, own_key, smallest, high):
    shape = entries.shape
    place = [jax.random.randint(jax.random.fold_in(own_key, axis), (), 0, shape[axis]) for axis in range(len(shape))]
    entries = entries.at[tuple(place)].set(smallest)
    longest = shape.index(max(shape))
    place[longest] = (place[longest] + 1) % shape[longest]
    return entries.at[tuple(place)].set(high)


def level_of(own_key, shape, cuts, least, high):
    level = 1.0
    for axis_at, parts in cuts:
        steps = jax.random.uniform(jax.random.fold_in(jax.random.fold_in(own_key, 6), axis_at), (parts,), jnp.float32, least / len(cuts), high / len(cuts))
        level = level * jnp.repeat(jnp.exp(steps), shape[axis_at] // parts).reshape((-1,) + (1,) * (len(shape) - 1 - axis_at))
    return level


def noise(rng, shape, scale, reach, split=(), kind=jnp.bfloat16):
    values = scale * jax.random.normal(rng, shape, jnp.float32)
    if split:
        values = values * level_of(rng, shape, split, -0.22, 0.18)
    return jnp.clip(values, -reach, reach).astype(kind)


def setup_inputs(seed: int = 0) -> dict:
    arg_keys = jax.random.split(jax.random.key(seed), 20)
    return {
        "atm_state": noise(arg_keys[0], (NLAT, NLON, C), 1.0, 6.0, ((0, 16), (1, 16))),
        "ocean_state": noise(arg_keys[1], (NLAT, NLON, OC), 1.0, 6.0, ((0, 32), (1, 8))),
        "wet_mask": with_ends((jax.random.randint(arg_keys[2], (NLAT, NLON), 0, 3) < 2).astype(jnp.int32), jax.random.fold_in(arg_keys[2], 1), 0, 1),
        "legendre": noise(arg_keys[3], (MODES, DEG, NLAT), 1.0, 4.0, ((0, 256),)),
        "quad_weight": jnp.clip(jnp.exp(jax.random.uniform(arg_keys[4], (NLAT,), jnp.float32, math.log(0.5), math.log(2.0))), 0.5, 2.0),
        "spec_real": noise(arg_keys[5], (C, C), C ** -0.5, 0.3125),
        "spec_imag": noise(arg_keys[6], (C, C), C ** -0.5, 0.3125),
        "degree_gain": jnp.clip(jnp.exp(jax.random.uniform(arg_keys[7], (DEG,), jnp.float32, math.log(0.5), math.log(2.0))), 0.5, 2.0),
        "atm_gain": jnp.clip(1.0 + 0.18 * jax.random.normal(arg_keys[8], (2, C), jnp.float32), 0.1, 1.9),
        "atm_up": noise(arg_keys[9], (C, HID), C ** -0.5, 0.3125),
        "atm_down": noise(arg_keys[10], (HID, C), HID ** -0.5, 0.21875),
        "atm_to_surface": noise(arg_keys[11], (C, SURF), C ** -0.5, 0.3125),
        "surface_to_atm": noise(arg_keys[12], (SURF, C), SURF ** -0.5, 1.0),
        "ocean_to_surface": noise(arg_keys[13], (OC, SURF), OC ** -0.5, 0.375),
        "surface_to_ocean": noise(arg_keys[14], (SURF, OC), SURF ** -0.5, 1.0),
        "ocean_kernel": noise(arg_keys[15], (2, STENCIL_TAPS, STENCIL_TAPS, OC), (STENCIL_TAPS * STENCIL_TAPS) ** -0.5, 0.875),
        "ocean_gain": jnp.clip(1.0 + 0.18 * jax.random.normal(arg_keys[16], (2, OC), jnp.float32), 0.1, 1.9),
        "ocean_up": noise(arg_keys[17], (2, OC, OHID), OC ** -0.5, 0.375),
        "ocean_down": noise(arg_keys[18], (2, OHID, OC), OHID ** -0.5, 0.1875),
    }


epsilon = 1e-05

def layer_norm(values, gain):
    centred = values - lax.optimization_barrier(jnp.mean(values, axis=-1, keepdims=True))
    spread = lax.optimization_barrier(jnp.mean(centred * centred, axis=-1, keepdims=True))
    return centred * lax.rsqrt(spread + epsilon) * gain

def wave_table(row_index, circle):
    longitude = jnp.arange(circle, dtype=jnp.int32)
    wavenumber = row_index // 2
    phases = wavenumber[:, None] * longitude[None, :] % circle
    angles = phases.astype(jnp.float32) * (2.0 * math.pi / circle)
    waves = jnp.where((row_index % 2 == 0)[:, None], jnp.cos(angles), -jnp.sin(angles))
    return (wavenumber, waves)

def forward_table(row_index, circle):
    wavenumber, waves = wave_table(row_index, circle)
    return (waves.T / math.sqrt(circle)).astype(jnp.bfloat16)

def inverse_table(row_index, circle):
    wavenumber, waves = wave_table(row_index, circle)
    factor = jnp.where(wavenumber == 0, 1.0, 2.0).astype(jnp.float32)
    return (waves * factor[:, None] / math.sqrt(circle)).astype(jnp.bfloat16)

def spectral_filter(gathered, table, quad_weight, spec_real, spec_imag, degree_gain):
    count = table.shape[0]
    lat_total = table.shape[2]
    channels = gathered.shape[2]
    split_parts = gathered.reshape(lat_total, count, 2, channels)
    weighted = (table.astype(jnp.float32) * (quad_weight / lat_total)).astype(jnp.bfloat16)
    coeffs = jnp.einsum('mln,nmpc->mplc', weighted.astype(jnp.float32), split_parts.astype(jnp.float32)).astype(jnp.bfloat16)
    real_part = coeffs[:, 0]
    imag_part = coeffs[:, 1]
    mixed_real = jnp.dot(real_part, spec_real, preferred_element_type=jnp.float32) - jnp.dot(imag_part, spec_imag, preferred_element_type=jnp.float32)
    mixed_imag = jnp.dot(real_part, spec_imag, preferred_element_type=jnp.float32) + jnp.dot(imag_part, spec_real, preferred_element_type=jnp.float32)
    scaled = (jnp.stack([mixed_real, mixed_imag], axis=1) * degree_gain[:, None]).astype(jnp.bfloat16)
    returned = jnp.einsum('mln,mplc->nmpc', table.astype(jnp.float32), scaled.astype(jnp.float32)).astype(jnp.bfloat16)
    return returned.reshape(lat_total, 2 * count, channels)

def ocean_block(padded_field, kernel, gain, up_weight, down_weight):
    stencil_reach = STENCIL_TAPS // 2 * OCEAN_DILATION
    tile_height = padded_field.shape[0] - 2 * stencil_reach
    tile_breadth = padded_field.shape[1] - 2 * stencil_reach
    stencil = jnp.zeros((tile_height, tile_breadth, padded_field.shape[2]), jnp.float32)
    for row_offset_tap in range(STENCIL_TAPS):
        for column_tap in range(STENCIL_TAPS):
            stencil_window = padded_field[row_offset_tap * OCEAN_DILATION:row_offset_tap * OCEAN_DILATION + tile_height, column_tap * OCEAN_DILATION:column_tap * OCEAN_DILATION + tile_breadth]
            stencil = stencil + stencil_window.astype(jnp.float32) * kernel[row_offset_tap, column_tap].astype(jnp.float32)
    normed = layer_norm(stencil, gain).astype(jnp.bfloat16)
    hidden = jax.nn.gelu(jnp.dot(normed, up_weight, preferred_element_type=jnp.float32)).astype(jnp.bfloat16)
    centre = padded_field[stencil_reach:stencil_reach + tile_height, stencil_reach:stencil_reach + tile_breadth]
    return (centre.astype(jnp.float32) + jnp.dot(hidden, down_weight, preferred_element_type=jnp.float32)).astype(jnp.bfloat16)

def ocean_layer(state, kernel, gain, up_weight, down_weight):
    stencil_reach = STENCIL_TAPS // 2 * OCEAN_DILATION
    padded_field = jnp.pad(state, ((stencil_reach, stencil_reach), (stencil_reach, stencil_reach), (0, 0)))

    def one_band(band_index):
        start = (band_index * LAT_DEV).astype(jnp.int32)
        piece = lax.dynamic_slice_in_dim(padded_field, start, LAT_DEV + 2 * stencil_reach, 0)
        return ocean_block(piece, kernel, gain, up_weight, down_weight)
    bands = lax.map(one_band, jnp.arange(N_LAT, dtype=jnp.int32))
    return bands.reshape(NLAT, NLON, OC)

def reference(atm_state, ocean_state, wet_mask, legendre, quad_weight, spec_real, spec_imag, degree_gain, atm_gain, atm_up, atm_down, atm_to_surface, surface_to_atm, ocean_to_surface, surface_to_ocean, ocean_kernel, ocean_gain, ocean_up, ocean_down):
    wet = wet_mask.astype(jnp.float32)[:, :, None]
    ocean_flux = (jnp.dot(ocean_state, ocean_to_surface, preferred_element_type=jnp.float32) * wet).astype(jnp.bfloat16)
    forced = atm_state.astype(jnp.float32) + jnp.dot(ocean_flux, surface_to_atm, preferred_element_type=jnp.float32)
    normed = layer_norm(forced, atm_gain[0]).astype(jnp.bfloat16)
    row_index = jnp.arange(2 * MODES, dtype=jnp.int32)
    forward = forward_table(row_index, NLON)
    inverse = inverse_table(row_index, NLON)

    def to_spectrum(lat_band):
        return jnp.einsum('anc,nr->arc', lat_band.astype(jnp.float32), forward.astype(jnp.float32)).astype(jnp.bfloat16)
    spectrum = lax.map(to_spectrum, normed.reshape(N_LAT, LAT_DEV, NLON, C))
    spectrum = spectrum.reshape(NLAT, DEVICES, 2 * MODES_DEV, C)
    owner_blocks = jnp.moveaxis(spectrum, 1, 0)
    table_blocks = legendre.reshape(DEVICES, MODES_DEV, DEG, NLAT)

    def one_owner(pieces):
        return spectral_filter(pieces[0], pieces[1], quad_weight, spec_real, spec_imag, degree_gain)
    filtered = lax.map(one_owner, (owner_blocks, table_blocks))
    returned = jnp.moveaxis(filtered, 0, 1).reshape(N_LAT, LAT_DEV, 2 * MODES, C)

    def finish(pieces):
        lat_band, forced_band = pieces
        spatial = jnp.einsum('arc,rn->anc', lat_band.astype(jnp.float32), inverse.astype(jnp.float32)).astype(jnp.bfloat16)
        mixed = forced_band + spatial.astype(jnp.float32)
        normed_two = layer_norm(mixed, atm_gain[1]).astype(jnp.bfloat16)
        hidden = jax.nn.gelu(jnp.dot(normed_two, atm_up, preferred_element_type=jnp.float32)).astype(jnp.bfloat16)
        return (mixed + jnp.dot(hidden, atm_down, preferred_element_type=jnp.float32)).astype(jnp.bfloat16)
    atm_out = lax.map(finish, (returned, forced.reshape(N_LAT, LAT_DEV, NLON, C))).reshape(NLAT, NLON, C)
    atm_flux = jnp.dot(atm_state, atm_to_surface, preferred_element_type=jnp.float32).astype(jnp.bfloat16)
    current = (ocean_state.astype(jnp.float32) + wet * jnp.dot(atm_flux, surface_to_ocean, preferred_element_type=jnp.float32)).astype(jnp.bfloat16)
    for block_index in range(2):
        current = ocean_layer(current, ocean_kernel[block_index], ocean_gain[block_index], ocean_up[block_index], ocean_down[block_index])
    ocean_out = jnp.where(wet_mask[:, :, None] == 1, current, ocean_state)
    return (atm_out, ocean_out)
```

```python
import math

import jax
import jax.numpy as jnp
import ml_dtypes
import numpy as np
from jax import lax
from jax.experimental import pallas as pl
from jax.experimental.pallas import tpu as pltpu
from jax.sharding import PartitionSpec as P

MODES = 512
STENCIL_TAPS = 7
OCEAN_DILATION = 2
LON_COMP = ("lon", "comp")
LON = ("lon",)
LAT_LON = ("lat", "lon")


epsilon = 1e-05


def padded(block, sides, width):
    for axis, dim in sides:
        count = lax.axis_size(axis)
        forward = [(i, i + 1) for i in range(count - 1)]
        backward = [(target, source) for source, target in forward]
        low = lax.ppermute(
            lax.slice_in_dim(block, block.shape[dim] - width, None, axis=dim), axis, forward
        )
        high = lax.ppermute(lax.slice_in_dim(block, 0, width, axis=dim), axis, backward)
        block = jnp.concatenate([low, block, high], axis=dim)
    return block


def layer_norm(values, gain):
    centred = values - jnp.mean(values, axis=-1, keepdims=True)
    spread = jnp.mean(centred * centred, axis=-1, keepdims=True)
    return centred * lax.rsqrt(spread + epsilon) * gain


def wave_tables(lat_count, lon_count, circle, owned):
    rows = np.arange(lat_count * lon_count * owned)
    block = circle // (2 * lon_count)
    where = np.arange(lon_count * block)
    forward, inverse = [], []
    row_sets = [rows // owned * 2 * owned + q * owned + rows % owned for q in range(2)]
    place_sets = [(where // block * 2 + q) * block + where % block for q in range(2)]

    def waves(row, place):
        phase = (row[:, None] // 2) * place[None, :] % circle
        angle = phase.astype(np.float32) * np.float32(2.0 * math.pi / circle)
        return np.where((row % 2 == 0)[:, None], np.cos(angle), -np.sin(angle)).astype(np.float32)

    for own in range(2):
        order = (own, 1 - own)
        f = np.concatenate([waves(row_sets[own], place_sets[q]) for q in order], 1)
        forward.append(f / np.float32(math.sqrt(circle)))
        g = []
        for q in order:
            factor = np.where(row_sets[q] // 2 == 0, 1.0, 2.0).astype(np.float32)
            g.append((waves(row_sets[q], place_sets[own]) * factor[:, None]).T)
        inverse.append(np.concatenate(g, 1) / np.float32(math.sqrt(circle)))
    return (
        np.stack(forward).astype(ml_dtypes.bfloat16),
        np.stack(inverse).astype(ml_dtypes.bfloat16),
    )


def forward_kernel(table_ref, own_ref, other_ref, out_ref):
    groups, lats, span, width = own_ref.shape
    half = groups * span
    for i in range(lats):
        total = jnp.dot(
            table_ref[:, :half],
            own_ref[:, i].reshape(half, width),
            preferred_element_type=jnp.float32,
        ) + jnp.dot(
            table_ref[:, half:],
            other_ref[:, i].reshape(half, width),
            preferred_element_type=jnp.float32,
        )
        out_ref[:, i] = total.astype(jnp.bfloat16).reshape(
            out_ref.shape[0], out_ref.shape[2], width
        )


def inverse_kernel(table_ref, own_ref, other_ref, out_ref):
    owners, lats, owned, width = own_ref.shape
    half = owners * owned
    for i in range(lats):
        total = jnp.dot(
            table_ref[:, :half],
            own_ref[:, i].reshape(half, width),
            preferred_element_type=jnp.float32,
        ) + jnp.dot(
            table_ref[:, half:],
            other_ref[:, i].reshape(half, width),
            preferred_element_type=jnp.float32,
        )
        out_ref[:, i] = total.astype(jnp.bfloat16).reshape(
            out_ref.shape[0], out_ref.shape[2], width
        )


def filter_kernel(
    weighted_ref, turned_ref, spectrum_ref, real_ref, imag_ref, gain_ref, out_ref, rows_ref
):
    count = weighted_ref.shape[0]
    lats, owned, width = spectrum_ref.shape
    block = 64
    side = block * owned
    r = lax.broadcasted_iota(jnp.int32, (side, side), 0)
    s = lax.broadcasted_iota(jnp.int32, (side, side), 1)
    pick = jnp.where((r % block) * owned + r // block == s, 1.0, 0.0).astype(jnp.bfloat16)
    back = jnp.where((s % block) * owned + s // block == r, 1.0, 0.0).astype(jnp.bfloat16)
    for b in range(lats // block):
        piece = spectrum_ref[b * block : (b + 1) * block].reshape(side, width)
        moved = jnp.dot(pick, piece, preferred_element_type=jnp.float32).astype(jnp.bfloat16)
        for p in range(owned):
            rows_ref[p, b * block : (b + 1) * block] = moved[p * block : (p + 1) * block]
    real, imag, gain = real_ref[...], imag_ref[...], gain_ref[...]
    for m in range(count):
        parts = [
            jnp.dot(
                weighted_ref[m], rows_ref[2 * m + q], preferred_element_type=jnp.float32
            ).astype(jnp.bfloat16)
            for q in range(2)
        ]
        mixed_real = jnp.dot(parts[0], real, preferred_element_type=jnp.float32) - jnp.dot(
            parts[1], imag, preferred_element_type=jnp.float32
        )
        mixed_imag = jnp.dot(parts[0], imag, preferred_element_type=jnp.float32) + jnp.dot(
            parts[1], real, preferred_element_type=jnp.float32
        )
        for q, mixed in enumerate((mixed_real, mixed_imag)):
            filtered = (mixed * gain).astype(jnp.bfloat16)
            rows_ref[2 * m + q] = jnp.dot(
                turned_ref[m], filtered, preferred_element_type=jnp.float32
            ).astype(jnp.bfloat16)
    for b in range(lats // block):
        piece = jnp.concatenate(
            [rows_ref[p, b * block : (b + 1) * block] for p in range(owned)], axis=0
        )
        moved = jnp.dot(back, piece, preferred_element_type=jnp.float32).astype(jnp.bfloat16)
        out_ref[b * block : (b + 1) * block] = moved.reshape(block, owned, width)


def call(kernel, shape, *args, scratch=(), limit=48):
    return pl.pallas_call(
        kernel,
        out_shape=jax.ShapeDtypeStruct(shape, jnp.bfloat16),
        in_specs=[pl.BlockSpec(memory_space=pltpu.VMEM)] * len(args),
        out_specs=pl.BlockSpec(memory_space=pltpu.VMEM),
        scratch_shapes=list(scratch),
        compiler_params=pltpu.CompilerParams(vmem_limit_bytes=limit * 2**20),
    )(*args)


def ocean_block(padded_field, kernel, gain, up_weight, down_weight):
    stencil_reach = STENCIL_TAPS // 2 * OCEAN_DILATION
    tile_height = padded_field.shape[0] - 2 * stencil_reach
    tile_breadth = padded_field.shape[1] - 2 * stencil_reach
    stencil = jnp.zeros((tile_height, tile_breadth, padded_field.shape[2]), jnp.float32)
    for row_offset_tap in range(STENCIL_TAPS):
        for column_tap in range(STENCIL_TAPS):
            stencil_window = padded_field[
                row_offset_tap * OCEAN_DILATION : row_offset_tap * OCEAN_DILATION + tile_height,
                column_tap * OCEAN_DILATION : column_tap * OCEAN_DILATION + tile_breadth,
            ]
            stencil = stencil + stencil_window.astype(jnp.float32) * kernel[
                row_offset_tap, column_tap
            ].astype(jnp.float32)
    normed = layer_norm(stencil, gain).astype(jnp.bfloat16)
    hidden = jax.nn.gelu(jnp.dot(normed, up_weight, preferred_element_type=jnp.float32)).astype(
        jnp.bfloat16
    )
    centre = padded_field[
        stencil_reach : stencil_reach + tile_height, stencil_reach : stencil_reach + tile_breadth
    ]
    return (
        centre.astype(jnp.float32)
        + jnp.dot(hidden, down_weight, preferred_element_type=jnp.float32)
    ).astype(jnp.bfloat16)


def local(
    atm_state,
    ocean_state,
    wet_mask,
    legendre,
    quad_weight,
    spec_real,
    spec_imag,
    degree_gain,
    atm_gain,
    atm_up,
    atm_down,
    atm_to_surface,
    surface_to_atm,
    ocean_to_surface,
    surface_to_ocean,
    ocean_kernel,
    ocean_gain,
    ocean_up,
    ocean_down,
):
    lat_count = lax.axis_size("lat")
    lon_count = lax.axis_size("lon")
    lat_dev, lon_dev, width = atm_state.shape
    sea_rows, sea_cols, sea_width = ocean_state.shape
    lat_total = lat_dev * lat_count
    circle = lon_dev * lon_count * 2
    owned = 2 * legendre.shape[0]
    owners = lat_count * lon_count
    lats = lat_dev // lon_count
    me = lax.axis_index("comp")
    swap = [(0, 1), (1, 0)]
    forward, inverse = wave_tables(lat_count, lon_count, circle, owned)
    forward = lax.dynamic_index_in_dim(jnp.asarray(forward), me, 0, keepdims=False)
    inverse = lax.dynamic_index_in_dim(jnp.asarray(inverse), me, 0, keepdims=False)
    wet = wet_mask.astype(jnp.float32)[:, :, None]
    ocean_flux = (
        jnp.dot(ocean_state, ocean_to_surface, preferred_element_type=jnp.float32) * wet
    ).astype(jnp.bfloat16)
    atm_flux = jnp.dot(atm_state, atm_to_surface, preferred_element_type=jnp.float32).astype(
        jnp.bfloat16
    )

    def across(mine, dim):
        pieces = jnp.split(mine, 2, axis=dim)
        kept = jnp.where(me == 0, pieces[0], pieces[1])
        got = lax.ppermute(jnp.where(me == 0, pieces[1], pieces[0]), "comp", swap)
        low = jnp.where(me == 0, kept, got)
        high = jnp.where(me == 0, got, kept)
        return jnp.concatenate([low, high], axis=1 - dim)

    flux_here = across(ocean_flux, 1)
    flux_sea = across(atm_flux, 0)
    forced = atm_state.astype(jnp.float32) + jnp.dot(
        flux_here, surface_to_atm, preferred_element_type=jnp.float32
    )
    normed = layer_norm(forced, atm_gain[0]).astype(jnp.bfloat16)
    rings = lax.all_to_all(
        normed.reshape(lon_count, lats, lon_dev, width), "lon", 0, 0, tiled=True
    )
    weighted = (legendre.astype(jnp.float32) * (quad_weight / lat_total)).astype(jnp.bfloat16)
    turned = jnp.swapaxes(legendre, 1, 2)
    spectrum = call(
        forward_kernel,
        (owners, lats, owned, width),
        forward,
        rings,
        lax.ppermute(rings, "comp", swap),
    )
    gathered = lax.all_to_all(spectrum, LAT_LON, 0, 0, tiled=True)
    filtered = call(
        filter_kernel,
        (lat_total, owned, width),
        weighted,
        turned,
        gathered.reshape(lat_total, owned, width),
        spec_real,
        spec_imag,
        degree_gain[:, None],
        scratch=[pltpu.VMEM((owned, lat_total, width), jnp.bfloat16)],
    )
    returned = lax.all_to_all(
        filtered.reshape(owners, lats, owned, width), LAT_LON, 0, 0, tiled=True
    )
    spatial = call(
        inverse_kernel,
        (lon_count, lats, lon_dev, width),
        inverse,
        returned,
        lax.ppermute(returned, "comp", swap),
    )
    spectral = lax.all_to_all(spatial, "lon", 0, 0, tiled=True).reshape(lat_dev, lon_dev, width)
    mixed = forced + spectral.astype(jnp.float32)
    normed_two = layer_norm(mixed, atm_gain[1]).astype(jnp.bfloat16)
    hidden = jax.nn.gelu(jnp.dot(normed_two, atm_up, preferred_element_type=jnp.float32)).astype(
        jnp.bfloat16
    )
    atm_out = (mixed + jnp.dot(hidden, atm_down, preferred_element_type=jnp.float32)).astype(
        jnp.bfloat16
    )
    ocean_in = (
        ocean_state.astype(jnp.float32)
        + wet * jnp.dot(flux_sea, surface_to_ocean, preferred_element_type=jnp.float32)
    ).astype(jnp.bfloat16)
    stencil_reach = STENCIL_TAPS // 2 * OCEAN_DILATION
    padded_field = padded(ocean_in, ((("lat", "comp"), 0), (LON, 1)), 2 * stencil_reach)
    first = ocean_block(padded_field, ocean_kernel[0], ocean_gain[0], ocean_up[0], ocean_down[0])
    row_global = (
        lax.axis_index(("lat", "comp")) * sea_rows
        - stencil_reach
        + jnp.arange(sea_rows + 2 * stencil_reach, dtype=jnp.int32)
    )
    col_global = (
        lax.axis_index(LON) * sea_cols
        - stencil_reach
        + jnp.arange(sea_cols + 2 * stencil_reach, dtype=jnp.int32)
    )
    inside = ((row_global >= 0) & (row_global < lat_total))[:, None] & (
        (col_global >= 0) & (col_global < circle)
    )[None, :]
    first = jnp.where(inside[:, :, None], first, jnp.zeros((), jnp.bfloat16))
    current = ocean_block(first, ocean_kernel[1], ocean_gain[1], ocean_up[1], ocean_down[1])
    ocean_out = jnp.where(wet_mask[:, :, None] == 1, current, ocean_state)
    return (atm_out, ocean_out)


def solution(mesh):
    placed = (
        P("lat", LON_COMP, None),
        P(("lat", "comp"), LON, None),
        P(("lat", "comp"), LON),
        P(("lat", "lon", "comp"), None, None),
        P(),
        P(),
        P(),
        P(),
        P(),
        P(),
        P(),
        P(),
        P(),
        P(),
        P(),
        P(),
        P(),
        P(),
        P(),
    )
    return jax.shard_map(
        local,
        mesh=mesh,
        in_specs=placed,
        out_specs=(P("lat", LON_COMP, None), P(("lat", "comp"), LON, None)),
        check_vma=False,
    )
```

```python
import math

import jax
import jax.numpy as jnp
import ml_dtypes
import numpy as np
from jax import lax
from jax.experimental import pallas as pl
from jax.experimental.pallas import tpu as pltpu
from jax.sharding import PartitionSpec as P

MODES = 512
STENCIL_TAPS = 7
OCEAN_DILATION = 2
LON_COMP = ("lon", "comp")
LON = ("lon",)
LAT_LON = ("lat", "lon")


epsilon = 1e-05


def wave_tables(lat_count, lon_count, circle, owned):
    rows = np.arange(lat_count * lon_count * owned)
    block = circle // (2 * lon_count)
    where = np.arange(lon_count * block)
    forward, inverse = [], []
    row_sets = [rows // owned * 2 * owned + q * owned + rows % owned for q in range(2)]
    place_sets = [(where // block * 2 + q) * block + where % block for q in range(2)]

    def waves(row, place):
        phase = (row[:, None] // 2) * place[None, :] % circle
        angle = phase.astype(np.float32) * np.float32(2.0 * math.pi / circle)
        return np.where((row % 2 == 0)[:, None], np.cos(angle), -np.sin(angle)).astype(np.float32)

    for own in range(2):
        order = (own, 1 - own)
        f = np.concatenate([waves(row_sets[own], place_sets[q]) for q in order], 1)
        forward.append(f / np.float32(math.sqrt(circle)))
        g = []
        for q in order:
            factor = np.where(row_sets[q] // 2 == 0, 1.0, 2.0).astype(np.float32)
            g.append((waves(row_sets[q], place_sets[own]) * factor[:, None]).T)
        inverse.append(np.concatenate(g, 1) / np.float32(math.sqrt(circle)))
    return (
        np.stack(forward).astype(ml_dtypes.bfloat16),
        np.stack(inverse).astype(ml_dtypes.bfloat16),
    )


def forward_kernel(table_ref, own_ref, other_ref, out_ref):
    groups, lats, span, width = own_ref.shape
    half = groups * span
    for i in range(lats):
        total = jnp.dot(
            table_ref[:, :half],
            own_ref[:, i].reshape(half, width),
            preferred_element_type=jnp.float32,
        ) + jnp.dot(
            table_ref[:, half:],
            other_ref[:, i].reshape(half, width),
            preferred_element_type=jnp.float32,
        )
        out_ref[:, i] = total.astype(jnp.bfloat16).reshape(
            out_ref.shape[0], out_ref.shape[2], width
        )


def inverse_kernel(table_ref, own_ref, other_ref, out_ref):
    owners, lats, owned, width = own_ref.shape
    half = owners * owned
    for i in range(lats):
        total = jnp.dot(
            table_ref[:, :half],
            own_ref[:, i].reshape(half, width),
            preferred_element_type=jnp.float32,
        ) + jnp.dot(
            table_ref[:, half:],
            other_ref[:, i].reshape(half, width),
            preferred_element_type=jnp.float32,
        )
        out_ref[:, i] = total.astype(jnp.bfloat16).reshape(
            out_ref.shape[0], out_ref.shape[2], width
        )


def filter_kernel(
    weighted_ref, turned_ref, spectrum_ref, real_ref, imag_ref, gain_ref, out_ref, rows_ref
):
    count = weighted_ref.shape[0]
    lats, owned, width = spectrum_ref.shape
    block = 64
    side = block * owned
    r = lax.broadcasted_iota(jnp.int32, (side, side), 0)
    s = lax.broadcasted_iota(jnp.int32, (side, side), 1)
    pick = jnp.where((r % block) * owned + r // block == s, 1.0, 0.0).astype(jnp.bfloat16)
    back = jnp.where((s % block) * owned + s // block == r, 1.0, 0.0).astype(jnp.bfloat16)
    for b in range(lats // block):
        piece = spectrum_ref[b * block : (b + 1) * block].reshape(side, width)
        moved = jnp.dot(pick, piece, preferred_element_type=jnp.float32).astype(jnp.bfloat16)
        for p in range(owned):
            rows_ref[p, b * block : (b + 1) * block] = moved[p * block : (p + 1) * block]
    real, imag, gain = real_ref[...], imag_ref[...], gain_ref[...]
    for m in range(count):
        parts = [
            jnp.dot(
                weighted_ref[m], rows_ref[2 * m + q], preferred_element_type=jnp.float32
            ).astype(jnp.bfloat16)
            for q in range(2)
        ]
        mixed_real = jnp.dot(parts[0], real, preferred_element_type=jnp.float32) - jnp.dot(
            parts[1], imag, preferred_element_type=jnp.float32
        )
        mixed_imag = jnp.dot(parts[0], imag, preferred_element_type=jnp.float32) + jnp.dot(
            parts[1], real, preferred_element_type=jnp.float32
        )
        for q, mixed in enumerate((mixed_real, mixed_imag)):
            filtered = (mixed * gain).astype(jnp.bfloat16)
            rows_ref[2 * m + q] = jnp.dot(
                turned_ref[m], filtered, preferred_element_type=jnp.float32
            ).astype(jnp.bfloat16)
    for b in range(lats // block):
        piece = jnp.concatenate(
            [rows_ref[p, b * block : (b + 1) * block] for p in range(owned)], axis=0
        )
        moved = jnp.dot(back, piece, preferred_element_type=jnp.float32).astype(jnp.bfloat16)
        out_ref[b * block : (b + 1) * block] = moved.reshape(block, owned, width)


def call(kernel, shape, *args, scratch=(), limit=16, scalars=0):
    spaces = [pltpu.SMEM] * scalars + [pltpu.VMEM] * (len(args) - scalars)
    return pl.pallas_call(
        kernel,
        out_shape=jax.ShapeDtypeStruct(shape, jnp.bfloat16),
        in_specs=[pl.BlockSpec(memory_space=space) for space in spaces],
        out_specs=pl.BlockSpec(memory_space=pltpu.VMEM),
        scratch_shapes=list(scratch),
        compiler_params=pltpu.CompilerParams(vmem_limit_bytes=limit * 2**20),
    )(*args)


def gelu(x):
    inner = x * (math.sqrt(2.0 / math.pi) + (math.sqrt(2.0 / math.pi) * 0.044715) * (x * x))
    half = 0.5 * x
    return half + half * jnp.tanh(inner)


def normalised(values, gain):
    centred = values - jnp.mean(values, axis=-1, keepdims=True)
    spread = jnp.mean(centred * centred, axis=-1, keepdims=True)
    return (centred * lax.rsqrt(spread + epsilon) * gain).astype(jnp.bfloat16)


def prologue_kernel(atm_ref, flux_ref, out_weight_ref, gain_ref, normed_ref):
    rows, lon_dev, width = atm_ref.shape
    forced = atm_ref[...].reshape(rows * lon_dev, width).astype(jnp.float32) + jnp.dot(
        flux_ref[...], out_weight_ref[...], preferred_element_type=jnp.float32
    )
    normed_ref[...] = normalised(forced, gain_ref[...]).reshape(rows, lon_dev, width)


def epilogue_kernel(
    atm_ref, flux_ref, spectral_ref, out_weight_ref, gain_ref, up_ref, down_ref, out_ref
):
    rows, lon_dev, width = atm_ref.shape
    side = rows * lon_dev
    forced = atm_ref[...].reshape(side, width).astype(jnp.float32) + jnp.dot(
        flux_ref[...], out_weight_ref[...], preferred_element_type=jnp.float32
    )
    mixed = forced + spectral_ref[...].reshape(side, width).astype(jnp.float32)
    normed = normalised(mixed, gain_ref[...])
    hidden = gelu(jnp.dot(normed, up_ref[...], preferred_element_type=jnp.float32))
    total = mixed + jnp.dot(
        hidden.astype(jnp.bfloat16), down_ref[...], preferred_element_type=jnp.float32
    )
    out_ref[...] = total.astype(jnp.bfloat16).reshape(rows, lon_dev, width)


def by_rows(kernel, atm, flux, spectral, weights, rows=4):
    lat_dev, lon_dev, width = atm.shape
    field = pl.BlockSpec((rows, lon_dev, width), lambda i: (i, 0, 0))
    fields = [atm, flux] + ([] if spectral is None else [spectral])
    specs = [field, pl.BlockSpec((rows * lon_dev, flux.shape[1]), lambda i: (i, 0))]
    specs += [] if spectral is None else [field]
    specs += [pl.BlockSpec(w.shape, lambda i: (0, 0)) for w in weights]
    return pl.pallas_call(
        kernel,
        grid=(lat_dev // rows,),
        out_shape=jax.ShapeDtypeStruct(atm.shape, jnp.bfloat16),
        in_specs=specs,
        out_specs=field,
        compiler_params=pltpu.CompilerParams(vmem_limit_bytes=16 * 2**20),
    )(*fields, *weights)


HALO = 16
LEAD = 8
LANES = 128
REACH = STENCIL_TAPS // 2 * OCEAN_DILATION


def ocean_rows(field, kern, gain, up, down, sums, out_ref, group, edges):
    blocks = field.shape[0]
    rows, cols, width = out_ref.shape
    stride = cols // 8
    each = stride // OCEAN_DILATION

    def step(g, carry):
        top = g * group
        for r in range(group):
            for lane in range(blocks):
                part = slice(lane * LANES, (lane + 1) * LANES)
                for parity in range(OCEAN_DILATION):
                    acc = [None] * each
                    for a in range(STENCIL_TAPS):
                        row = top + r + a * OCEAN_DILATION
                        first = LEAD - REACH + parity
                        loads = [
                            field[lane, row, pl.ds(first + OCEAN_DILATION * q, 8, stride=stride), :]
                            for q in range(each + STENCIL_TAPS - 1)
                        ]
                        for b in range(STENCIL_TAPS):
                            weight = kern[a * STENCIL_TAPS + b, :, part]
                            for q in range(each):
                                term = loads[q + b] * weight
                                acc[q] = term if acc[q] is None else acc[q] + term
                    for q in range(each):
                        at = pl.ds(parity + OCEAN_DILATION * q, 8, stride=stride)
                        sums[lane, r, at, :] = acc[q]
        side = group * cols
        stencil = jnp.concatenate(
            [sums[lane].reshape(side, LANES) for lane in range(blocks)], axis=1
        )
        normed = normalised(stencil, gain[...])
        hidden = gelu(jnp.dot(normed, up[...], preferred_element_type=jnp.float32))
        total = jnp.dot(
            hidden.astype(jnp.bfloat16), down[...], preferred_element_type=jnp.float32
        )
        for r in range(group):
            centre = jnp.concatenate(
                [field[lane, top + r + REACH, LEAD : LEAD + cols, :] for lane in range(blocks)],
                axis=1,
            )
            value = centre + total[r * cols : (r + 1) * cols]
            if edges is not None:
                row = edges[0] + top + r
                low, high = -edges[2], edges[3] - edges[2]
                high = jnp.where((row >= 0) & (row < edges[1]), high, low)
                col = lax.broadcasted_iota(jnp.int32, value.shape, 0)
                value = jnp.where((col >= low) & (col < high), value, 0.0)
            out_ref[top + r] = value.astype(jnp.bfloat16)
        return carry

    lax.fori_loop(0, rows // group, step, 0)


def first_ocean_kernel(
    edges_ref,
    centre_ref,
    north_ref,
    south_ref,
    west_ref,
    east_ref,
    nw_ref,
    ne_ref,
    sw_ref,
    se_ref,
    kern_ref,
    gain_ref,
    up_ref,
    down_ref,
    out_ref,
    field,
    sums,
):
    rows, cols, width = centre_ref.shape
    columns = (slice(0, HALO), slice(HALO, HALO + cols), slice(HALO + cols, cols + 2 * HALO))
    grid = (
        (nw_ref, north_ref, ne_ref),
        (west_ref, centre_ref, east_ref),
        (sw_ref, south_ref, se_ref),
    )
    for y, line in enumerate(grid):
        for x, ref in enumerate(line):
            for lane in range(width // LANES):
                field[lane, y * rows : (y + 1) * rows, columns[x], :] = ref[
                    :, :, lane * LANES : (lane + 1) * LANES
                ].astype(jnp.float32)
    edges = [edges_ref[n] for n in range(4)]
    ocean_rows(field, kern_ref, gain_ref, up_ref, down_ref, sums, out_ref, sums.shape[1], edges)


def second_ocean_kernel(
    first_ref, kern_ref, gain_ref, up_ref, down_ref, out_ref, field, sums
):
    for lane in range(field.shape[0]):
        field[lane] = first_ref[:, :, lane * LANES : (lane + 1) * LANES].astype(jnp.float32)
    ocean_rows(field, kern_ref, gain_ref, up_ref, down_ref, sums, out_ref, sums.shape[1], None)


def shifted(block, dy, dx):
    axes = ("lat", "lon", "comp")
    tall = lax.axis_size("lat") * lax.axis_size("comp")
    broad = lax.axis_size("lon")

    def place(y, x):
        return (y // 2 * broad + x) * 2 + y % 2

    pairs = [
        (place(y, x), place(y + dy, x + dx))
        for y in range(tall)
        for x in range(broad)
        if 0 <= y + dy < tall and 0 <= x + dx < broad
    ]
    return lax.ppermute(block, axes, pairs)


def local(
    atm_state,
    ocean_state,
    wet_mask,
    legendre,
    quad_weight,
    spec_real,
    spec_imag,
    degree_gain,
    atm_gain,
    atm_up,
    atm_down,
    atm_to_surface,
    surface_to_atm,
    ocean_to_surface,
    surface_to_ocean,
    ocean_kernel,
    ocean_gain,
    ocean_up,
    ocean_down,
):
    lat_count = lax.axis_size("lat")
    lon_count = lax.axis_size("lon")
    lat_dev, lon_dev, width = atm_state.shape
    sea_rows, sea_cols, sea_width = ocean_state.shape
    lat_total = lat_dev * lat_count
    circle = lon_dev * lon_count * 2
    owned = 2 * legendre.shape[0]
    owners = lat_count * lon_count
    lats = lat_dev // lon_count
    me = lax.axis_index("comp")
    swap = [(0, 1), (1, 0)]
    forward, inverse = wave_tables(lat_count, lon_count, circle, owned)
    forward = lax.dynamic_index_in_dim(jnp.asarray(forward), me, 0, keepdims=False)
    inverse = lax.dynamic_index_in_dim(jnp.asarray(inverse), me, 0, keepdims=False)
    wet = wet_mask.astype(jnp.float32)[:, :, None]
    ocean_flux = (
        jnp.dot(ocean_state, ocean_to_surface, preferred_element_type=jnp.float32) * wet
    ).astype(jnp.bfloat16)
    atm_flux = jnp.dot(atm_state, atm_to_surface, preferred_element_type=jnp.float32).astype(
        jnp.bfloat16
    )

    def halves(mine, dim):
        low, high = jnp.split(mine, 2, axis=dim)
        return (jnp.where(me == 0, low, high), jnp.where(me == 0, high, low))

    def together(kept, got, dim):
        low = jnp.where(me == 0, kept, got)
        high = jnp.where(me == 0, got, kept)
        return jnp.concatenate([low, high], axis=dim)

    kept_ocean, sent_ocean = halves(ocean_flux, 1)
    kept_atm, sent_atm = halves(atm_flux, 0)
    got = lax.ppermute(jnp.stack([sent_ocean, sent_atm]), "comp", swap)
    flux_here = together(kept_ocean, got[0], 0).reshape(lat_dev * lon_dev, -1)
    flux_sea = together(kept_atm, got[1], 1)
    normed = by_rows(
        prologue_kernel, atm_state, flux_here, None, (surface_to_atm, atm_gain[:1])
    )
    ocean_in = (
        ocean_state.astype(jnp.float32)
        + wet * jnp.dot(flux_sea, surface_to_ocean, preferred_element_type=jnp.float32)
    ).astype(jnp.bfloat16)
    normed, ocean_in = lax.optimization_barrier((normed, ocean_in))
    rings = lax.all_to_all(
        normed.reshape(lon_count, lats, lon_dev, width), "lon", 0, 0, tiled=True
    )
    west, east = ocean_in[:, -HALO:], ocean_in[:, :HALO]
    pieces = (
        shifted(ocean_in, 1, 0),
        shifted(ocean_in, -1, 0),
        shifted(west, 0, 1),
        shifted(east, 0, -1),
        shifted(west, 1, 1),
        shifted(east, 1, -1),
        shifted(west, -1, 1),
        shifted(east, -1, -1),
    )
    rings, pieces = lax.optimization_barrier((rings, pieces))
    weighted = (legendre.astype(jnp.float32) * (quad_weight / lat_total)).astype(jnp.bfloat16)
    turned = jnp.swapaxes(legendre, 1, 2)
    spectrum = call(
        forward_kernel,
        (owners, lats, owned, width),
        forward,
        rings,
        lax.ppermute(rings, "comp", swap),
    )
    spectrum, pieces = lax.optimization_barrier((spectrum, pieces))
    edges = jnp.stack(
        [
            lax.axis_index(("lat", "comp")) * sea_rows - REACH,
            jnp.int32(lat_total),
            lax.axis_index("lon") * sea_cols - LEAD,
            jnp.int32(circle),
        ]
    ).astype(jnp.int32)
    kernels = jnp.broadcast_to(
        ocean_kernel.astype(jnp.float32).reshape(2, STENCIL_TAPS**2, 1, sea_width),
        (2, STENCIL_TAPS**2, 8, sea_width),
    )
    lanes = sea_width // LANES
    reached = (sea_rows + 2 * REACH, sea_cols + 2 * LEAD, sea_width)
    first = call(
        first_ocean_kernel,
        reached,
        edges,
        ocean_in,
        *pieces,
        kernels[0],
        ocean_gain[:1],
        ocean_up[0],
        ocean_down[0],
        scratch=[
            pltpu.VMEM((lanes, 3 * sea_rows, sea_cols + 2 * HALO, LANES), jnp.float32),
            pltpu.VMEM((lanes, 2, reached[1], LANES), jnp.float32),
        ],
        scalars=1,
    )
    gathered = lax.all_to_all(spectrum, LAT_LON, 0, 0, tiled=True)
    gathered, first = lax.optimization_barrier((gathered, first))
    filtered = call(
        filter_kernel,
        (lat_total, owned, width),
        weighted,
        turned,
        gathered.reshape(lat_total, owned, width),
        spec_real,
        spec_imag,
        degree_gain[:, None],
        scratch=[pltpu.VMEM((owned, lat_total, width), jnp.bfloat16)],
    )
    filtered, first = lax.optimization_barrier((filtered, first))
    current = call(
        second_ocean_kernel,
        (sea_rows, sea_cols, sea_width),
        first,
        kernels[1],
        ocean_gain[1:],
        ocean_up[1],
        ocean_down[1],
        scratch=[
            pltpu.VMEM((lanes, *reached[:2], LANES), jnp.float32),
            pltpu.VMEM((lanes, 2, sea_cols, LANES), jnp.float32),
        ],
    )
    returned = lax.all_to_all(
        filtered.reshape(owners, lats, owned, width), LAT_LON, 0, 0, tiled=True
    )
    returned, current = lax.optimization_barrier((returned, current))
    spatial = call(
        inverse_kernel,
        (lon_count, lats, lon_dev, width),
        inverse,
        returned,
        lax.ppermute(returned, "comp", swap),
    )
    spectral = lax.all_to_all(spatial, "lon", 0, 0, tiled=True).reshape(lat_dev, lon_dev, width)
    atm_out = by_rows(
        epilogue_kernel,
        atm_state,
        flux_here,
        spectral,
        (surface_to_atm, atm_gain[1:], atm_up, atm_down),
    )
    ocean_out = jnp.where(wet_mask[:, :, None] == 1, current, ocean_state)
    return (atm_out, ocean_out)


def solution(mesh):
    placed = (
        P("lat", LON_COMP, None),
        P(("lat", "comp"), LON, None),
        P(("lat", "comp"), LON),
        P(("lat", "lon", "comp"), None, None),
        P(),
        P(),
        P(),
        P(),
        P(),
        P(),
        P(),
        P(),
        P(),
        P(),
        P(),
        P(),
        P(),
        P(),
        P(),
    )
    return jax.shard_map(
        local,
        mesh=mesh,
        in_specs=placed,
        out_specs=(P("lat", LON_COMP, None), P(("lat", "comp"), LON, None)),
        check_vma=False,
    )
```

```python
import math

import jax
import jax.numpy as jnp
import ml_dtypes
import numpy as np
from jax import lax
from jax.experimental import pallas as pl
from jax.experimental.pallas import tpu as pltpu
from jax.sharding import PartitionSpec as P

MODES = 512
STENCIL_TAPS = 7
OCEAN_DILATION = 2
LON_COMP = ("lon", "comp")
LON = ("lon",)
LAT_LON = ("lat", "lon")


epsilon = 1e-05


def wave_tables(lat_count, lon_count, circle, owned):
    rows = np.arange(lat_count * lon_count * owned)
    block = circle // (2 * lon_count)
    where = np.arange(lon_count * block)
    forward, inverse = [], []
    row_sets = [rows // owned * 2 * owned + q * owned + rows % owned for q in range(2)]
    place_sets = [(where // block * 2 + q) * block + where % block for q in range(2)]

    def waves(row, place):
        phase = (row[:, None] // 2) * place[None, :] % circle
        angle = phase.astype(np.float32) * np.float32(2.0 * math.pi / circle)
        return np.where((row % 2 == 0)[:, None], np.cos(angle), -np.sin(angle)).astype(np.float32)

    for own in range(2):
        order = (own, 1 - own)
        f = np.concatenate([waves(row_sets[own], place_sets[q]) for q in order], 1)
        forward.append(f / np.float32(math.sqrt(circle)))
        g = []
        for q in order:
            factor = np.where(row_sets[q] // 2 == 0, 1.0, 2.0).astype(np.float32)
            g.append((waves(row_sets[q], place_sets[own]) * factor[:, None]).T)
        inverse.append(np.concatenate(g, 1) / np.float32(math.sqrt(circle)))
    return (
        np.stack(forward).astype(ml_dtypes.bfloat16),
        np.stack(inverse).astype(ml_dtypes.bfloat16),
    )


def waves_kernel(
    table_hbm, own_hbm, other_hbm, out_hbm, table_ref, own_ref, other_ref, held, sems
):
    lats, width = own_ref.shape[0], own_ref.shape[3]
    half = table_ref.shape[1] // 2
    table = pltpu.make_async_copy(table_hbm, table_ref, sems.at[0])
    table.start()
    owns, others, sends = [], [], []
    for i in range(lats):
        owns.append(pltpu.make_async_copy(own_hbm.at[:, i], own_ref.at[i], sems.at[1 + i]))
        owns[-1].start()
        at = sems.at[1 + lats + i]
        others.append(pltpu.make_async_copy(other_hbm.at[:, i], other_ref.at[i], at))
        others[-1].start()
    table.wait()
    for i in range(lats):
        owns[i].wait()
        total = jnp.dot(
            table_ref[:, :half],
            own_ref[i].reshape(half, width),
            preferred_element_type=jnp.float32,
        )
        others[i].wait()
        total += jnp.dot(
            table_ref[:, half:],
            other_ref[i].reshape(half, width),
            preferred_element_type=jnp.float32,
        )
        held[i] = total.astype(jnp.bfloat16).reshape(held.shape[1:])
        at = sems.at[1 + 2 * lats + i]
        sends.append(pltpu.make_async_copy(held.at[i], out_hbm.at[:, i], at))
        sends[-1].start()
    for send in sends:
        send.wait()


def waves(shape, table, own, other):
    lats = shape[1]
    return call(
        waves_kernel,
        shape,
        table,
        own,
        other,
        scratch=[
            pltpu.VMEM(table.shape, jnp.bfloat16),
            pltpu.VMEM((lats, own.shape[0], *own.shape[2:]), jnp.bfloat16),
            pltpu.VMEM((lats, own.shape[0], *own.shape[2:]), jnp.bfloat16),
            pltpu.VMEM((lats, shape[0], *shape[2:]), jnp.bfloat16),
            pltpu.SemaphoreType.DMA((1 + 3 * lats,)),
        ],
        behind=3,
        away=True,
        room=1_300_000,
    )


def filter_kernel(
    gain_ref,
    spectrum_hbm,
    weighted_hbm,
    turned_hbm,
    real_hbm,
    imag_hbm,
    out_hbm,
    spectrum_ref,
    weighted_ref,
    turned_ref,
    real_ref,
    imag_ref,
    rows_ref,
    held,
    sems,
):
    count = weighted_ref.shape[0]
    lats, owned, width = spectrum_ref.shape
    block = 64
    side = block * owned
    parts = lats // block
    pairs = (
        (weighted_hbm, weighted_ref),
        (real_hbm, real_ref),
        (imag_hbm, imag_ref),
        (turned_hbm, turned_ref),
    )
    fetches = [
        pltpu.make_async_copy(source, target, sems.at[n])
        for n, (source, target) in enumerate(pairs)
    ]
    arrivals = []
    for b in range(parts):
        span = pl.ds(b * block, block)
        at = sems.at[len(pairs) + b]
        arrivals.append(pltpu.make_async_copy(spectrum_hbm.at[span], spectrum_ref.at[span], at))
        arrivals[-1].start()
    for fetch in fetches:
        fetch.start()
    r = lax.broadcasted_iota(jnp.int32, (side, side), 0)
    s = lax.broadcasted_iota(jnp.int32, (side, side), 1)
    pick = jnp.where((r % block) * owned + r // block == s, 1.0, 0.0).astype(jnp.bfloat16)
    back = jnp.where((s % block) * owned + s // block == r, 1.0, 0.0).astype(jnp.bfloat16)
    for b in range(parts):
        arrivals[b].wait()
        piece = spectrum_ref[b * block : (b + 1) * block].reshape(side, width)
        moved = jnp.dot(pick, piece, preferred_element_type=jnp.float32).astype(jnp.bfloat16)
        for p in range(owned):
            rows_ref[p, b * block : (b + 1) * block] = moved[p * block : (p + 1) * block]
    gain = jnp.transpose(jnp.broadcast_to(gain_ref[...], (8, lats)))[:, :1]
    for fetch in fetches:
        fetch.wait()
    real, imag = real_ref[...], imag_ref[...]
    for m in range(count):
        coeffs = [
            jnp.dot(
                weighted_ref[m], rows_ref[2 * m + q], preferred_element_type=jnp.float32
            ).astype(jnp.bfloat16)
            for q in range(2)
        ]
        mixed_real = jnp.dot(coeffs[0], real, preferred_element_type=jnp.float32) - jnp.dot(
            coeffs[1], imag, preferred_element_type=jnp.float32
        )
        mixed_imag = jnp.dot(coeffs[0], imag, preferred_element_type=jnp.float32) + jnp.dot(
            coeffs[1], real, preferred_element_type=jnp.float32
        )
        for q, mixed in enumerate((mixed_real, mixed_imag)):
            filtered = (mixed * gain).astype(jnp.bfloat16)
            rows_ref[2 * m + q] = jnp.dot(
                turned_ref[m], filtered, preferred_element_type=jnp.float32
            ).astype(jnp.bfloat16)
    sends = []
    for b in range(parts):
        piece = jnp.concatenate(
            [rows_ref[p, b * block : (b + 1) * block] for p in range(owned)], axis=0
        )
        moved = jnp.dot(back, piece, preferred_element_type=jnp.float32).astype(jnp.bfloat16)
        span = pl.ds(b * block, block)
        held[span] = moved.reshape(block, owned, width)
        sends.append(
            pltpu.make_async_copy(
                held.at[span], out_hbm.at[span], sems.at[len(pairs) + parts + b]
            )
        )
        sends[-1].start()
    for send in sends:
        send.wait()


VMEM = 62_900_000


def call(kernel, shape, *args, scratch=(), room=0, scalars=0, behind=0, away=False):
    spaces = [pltpu.SMEM] * scalars + [pltpu.VMEM] * (len(args) - scalars - behind)
    spaces += [pltpu.HBM] * behind
    return pl.pallas_call(
        kernel,
        out_shape=jax.ShapeDtypeStruct(shape, jnp.bfloat16),
        in_specs=[pl.BlockSpec(memory_space=space) for space in spaces],
        out_specs=pl.BlockSpec(memory_space=pltpu.HBM if away else pltpu.VMEM),
        scratch_shapes=list(scratch),
        compiler_params=pltpu.CompilerParams(vmem_limit_bytes=VMEM - room),
    )(*args)


def gelu(x):
    inner = x * (math.sqrt(2.0 / math.pi) + (math.sqrt(2.0 / math.pi) * 0.044715) * (x * x))
    half = 0.5 * x
    return half + half * jnp.tanh(inner)


def normalised(values, gain):
    centred = values - jnp.mean(values, axis=-1, keepdims=True)
    spread = jnp.mean(centred * centred, axis=-1, keepdims=True)
    return (centred * lax.rsqrt(spread + epsilon) * gain).astype(jnp.bfloat16)


def prologue_kernel(atm_ref, flux_ref, out_weight_ref, gain_ref, normed_ref):
    rows, lon_dev, width = atm_ref.shape
    forced = atm_ref[...].reshape(rows * lon_dev, width).astype(jnp.float32) + jnp.dot(
        flux_ref[...], out_weight_ref[...], preferred_element_type=jnp.float32
    )
    normed_ref[...] = normalised(forced, gain_ref[...]).reshape(rows, lon_dev, width)


def epilogue_kernel(
    atm_ref, flux_ref, spectral_ref, out_weight_ref, gain_ref, up_ref, down_ref, out_ref
):
    rows, lon_dev, width = atm_ref.shape
    side = rows * lon_dev
    forced = atm_ref[...].reshape(side, width).astype(jnp.float32) + jnp.dot(
        flux_ref[...], out_weight_ref[...], preferred_element_type=jnp.float32
    )
    mixed = forced + spectral_ref[...].reshape(side, width).astype(jnp.float32)
    normed = normalised(mixed, gain_ref[...])
    hidden = gelu(jnp.dot(normed, up_ref[...], preferred_element_type=jnp.float32))
    total = mixed + jnp.dot(
        hidden.astype(jnp.bfloat16), down_ref[...], preferred_element_type=jnp.float32
    )
    out_ref[...] = total.astype(jnp.bfloat16).reshape(rows, lon_dev, width)


def by_rows(kernel, atm, flux, spectral, weights, rows=4):
    lat_dev, lon_dev, width = atm.shape
    field = pl.BlockSpec((rows, lon_dev, width), lambda i: (i, 0, 0))
    fields = [atm, flux] + ([] if spectral is None else [spectral])
    specs = [field, pl.BlockSpec((rows * lon_dev, flux.shape[1]), lambda i: (i, 0))]
    specs += [] if spectral is None else [field]
    specs += [pl.BlockSpec(w.shape, lambda i: (0, 0)) for w in weights]
    return pl.pallas_call(
        kernel,
        grid=(lat_dev // rows,),
        out_shape=jax.ShapeDtypeStruct(atm.shape, jnp.bfloat16),
        in_specs=specs,
        out_specs=field,
        compiler_params=pltpu.CompilerParams(vmem_limit_bytes=VMEM - 100_000),
    )(*fields, *weights)


HALO = 16
LEAD = 8
LANES = 128
REACH = STENCIL_TAPS // 2 * OCEAN_DILATION


def ocean_rows(field, kern, gain, up, down, sums, out_ref, group, edges):
    blocks = field.shape[0]
    rows, cols, width = out_ref.shape
    stride = cols // 8
    each = stride // OCEAN_DILATION

    def step(g, carry):
        top = g * group
        for r in range(group):
            for lane in range(blocks):
                part = slice(lane * LANES, (lane + 1) * LANES)
                for parity in range(OCEAN_DILATION):
                    acc = [None] * each
                    for a in range(STENCIL_TAPS):
                        row = top + r + a * OCEAN_DILATION
                        first = LEAD - REACH + parity
                        loads = [
                            field[lane, row, pl.ds(first + OCEAN_DILATION * q, 8, stride=stride), :]
                            for q in range(each + STENCIL_TAPS - 1)
                        ]
                        for b in range(STENCIL_TAPS):
                            weight = kern[a * STENCIL_TAPS + b, :, part]
                            for q in range(each):
                                term = loads[q + b] * weight
                                acc[q] = term if acc[q] is None else acc[q] + term
                    for q in range(each):
                        at = pl.ds(parity + OCEAN_DILATION * q, 8, stride=stride)
                        sums[lane, r, at, :] = acc[q]
        side = group * cols
        stencil = jnp.concatenate(
            [sums[lane].reshape(side, LANES) for lane in range(blocks)], axis=1
        )
        normed = normalised(stencil, gain[...])
        hidden = gelu(jnp.dot(normed, up[...], preferred_element_type=jnp.float32))
        total = jnp.dot(
            hidden.astype(jnp.bfloat16), down[...], preferred_element_type=jnp.float32
        )
        for r in range(group):
            centre = jnp.concatenate(
                [field[lane, top + r + REACH, LEAD : LEAD + cols, :] for lane in range(blocks)],
                axis=1,
            )
            value = centre + total[r * cols : (r + 1) * cols]
            if edges is not None:
                row = edges[0] + top + r
                low, high = -edges[2], edges[3] - edges[2]
                high = jnp.where((row >= 0) & (row < edges[1]), high, low)
                col = lax.broadcasted_iota(jnp.int32, value.shape, 0)
                value = jnp.where((col >= low) & (col < high), value, 0.0)
            out_ref[top + r] = value.astype(jnp.bfloat16)
        return carry

    lax.fori_loop(0, rows // group, step, 0)


def first_ocean_kernel(
    edges_ref,
    centre_ref,
    north_ref,
    south_ref,
    kern_ref,
    gain_ref,
    up_ref,
    down_ref,
    out_ref,
    field,
    sums,
):
    rows, cols, width = centre_ref.shape
    for y, ref in enumerate((north_ref, centre_ref, south_ref)):
        for lane in range(width // LANES):
            field[lane, y * rows : (y + 1) * rows] = ref[
                :, :, lane * LANES : (lane + 1) * LANES
            ].astype(jnp.float32)
    edges = [edges_ref[n] for n in range(4)]
    ocean_rows(field, kern_ref, gain_ref, up_ref, down_ref, sums, out_ref, sums.shape[1], edges)


def second_ocean_kernel(
    first_ref, kern_ref, gain_ref, up_ref, down_ref, out_ref, field, sums
):
    for lane in range(field.shape[0]):
        field[lane] = first_ref[:, :, lane * LANES : (lane + 1) * LANES].astype(jnp.float32)
    ocean_rows(field, kern_ref, gain_ref, up_ref, down_ref, sums, out_ref, sums.shape[1], None)


def shifted(block, dy, dx):
    axes = ("lat", "lon", "comp")
    tall = lax.axis_size("lat") * lax.axis_size("comp")
    broad = lax.axis_size("lon")

    def place(y, x):
        return (y // 2 * broad + x) * 2 + y % 2

    pairs = [
        (place(y, x), place(y + dy, x + dx))
        for y in range(tall)
        for x in range(broad)
        if 0 <= y + dy < tall and 0 <= x + dx < broad
    ]
    return lax.ppermute(block, axes, pairs)


def local(
    atm_state,
    ocean_state,
    wet_mask,
    legendre,
    quad_weight,
    spec_real,
    spec_imag,
    degree_gain,
    atm_gain,
    atm_up,
    atm_down,
    atm_to_surface,
    surface_to_atm,
    ocean_to_surface,
    surface_to_ocean,
    ocean_kernel,
    ocean_gain,
    ocean_up,
    ocean_down,
):
    lat_count = lax.axis_size("lat")
    lon_count = lax.axis_size("lon")
    lat_dev, lon_dev, width = atm_state.shape
    sea_rows, sea_cols, sea_width = ocean_state.shape
    lat_total = lat_dev * lat_count
    circle = lon_dev * lon_count * 2
    owned = 2 * legendre.shape[0]
    owners = lat_count * lon_count
    lats = lat_dev // lon_count
    me = lax.axis_index("comp")
    swap = [(0, 1), (1, 0)]
    forward, inverse = wave_tables(lat_count, lon_count, circle, owned)
    forward = lax.dynamic_index_in_dim(jnp.asarray(forward), me, 0, keepdims=False)
    inverse = lax.dynamic_index_in_dim(jnp.asarray(inverse), me, 0, keepdims=False)
    wet = wet_mask.astype(jnp.float32)[:, :, None]
    ocean_flux = (
        jnp.dot(ocean_state, ocean_to_surface, preferred_element_type=jnp.float32) * wet
    ).astype(jnp.bfloat16)
    atm_flux = jnp.dot(atm_state, atm_to_surface, preferred_element_type=jnp.float32).astype(
        jnp.bfloat16
    )

    def halves(mine, dim):
        low, high = jnp.split(mine, 2, axis=dim)
        return (jnp.where(me == 0, low, high), jnp.where(me == 0, high, low))

    def together(kept, got, dim):
        low = jnp.where(me == 0, kept, got)
        high = jnp.where(me == 0, got, kept)
        return jnp.concatenate([low, high], axis=dim)

    kept_ocean, sent_ocean = halves(ocean_flux, 1)
    kept_atm, sent_atm = halves(atm_flux, 0)
    got_ocean = lax.ppermute(sent_ocean, "comp", swap)
    flux_here = together(kept_ocean, got_ocean, 0).reshape(lat_dev * lon_dev, -1)
    normed = by_rows(
        prologue_kernel, atm_state, flux_here, None, (surface_to_atm, atm_gain[:1])
    )
    rings = lax.all_to_all(
        normed.reshape(lon_count, lats, lon_dev, width), "lon", 0, 0, tiled=True
    )
    flux_sea = together(kept_atm, lax.ppermute(sent_atm, "comp", swap), 1)
    ocean_in = (
        ocean_state.astype(jnp.float32)
        + wet * jnp.dot(flux_sea, surface_to_ocean, preferred_element_type=jnp.float32)
    ).astype(jnp.bfloat16)
    west = shifted(ocean_in[:, -HALO:], 0, 1)
    east = shifted(ocean_in[:, :HALO], 0, -1)
    broad = jnp.concatenate([west, ocean_in, east], axis=1)
    rings, broad = lax.optimization_barrier((rings, broad))
    weighted = (legendre.astype(jnp.float32) * (quad_weight / lat_total)).astype(jnp.bfloat16)
    turned = jnp.swapaxes(legendre, 1, 2)
    spectrum = waves(
        (owners, lats, owned, width), forward, rings, lax.ppermute(rings, "comp", swap)
    )
    spectrum, broad = lax.optimization_barrier((spectrum, broad))
    gathered = lax.all_to_all(spectrum, LAT_LON, 0, 0, tiled=True)
    north = shifted(broad, 1, 0)
    south = shifted(broad, -1, 0)
    filtered = call(
        filter_kernel,
        (lat_total, owned, width),
        degree_gain[None],
        gathered.reshape(lat_total, owned, width),
        weighted,
        turned,
        spec_real,
        spec_imag,
        scratch=[
            pltpu.VMEM((lat_total, owned, width), jnp.bfloat16),
            pltpu.VMEM(weighted.shape, jnp.bfloat16),
            pltpu.VMEM(turned.shape, jnp.bfloat16),
            pltpu.VMEM(spec_real.shape, jnp.bfloat16),
            pltpu.VMEM(spec_imag.shape, jnp.bfloat16),
            pltpu.VMEM((owned, lat_total, width), jnp.bfloat16),
            pltpu.VMEM((lat_total, owned, width), jnp.bfloat16),
            pltpu.SemaphoreType.DMA((4 + lat_total // 64 * 2,)),
        ],
        behind=5,
        away=True,
        room=100_000,
    )
    filtered, north, south = lax.optimization_barrier((filtered, north, south))
    returned = lax.all_to_all(
        filtered.reshape(owners, lats, owned, width), LAT_LON, 0, 0, tiled=True
    )
    edges = jnp.stack(
        [
            lax.axis_index(("lat", "comp")) * sea_rows - REACH,
            jnp.int32(lat_total),
            lax.axis_index("lon") * sea_cols - LEAD,
            jnp.int32(circle),
        ]
    ).astype(jnp.int32)
    kernels = jnp.broadcast_to(
        ocean_kernel.astype(jnp.float32).reshape(2, STENCIL_TAPS**2, 1, sea_width),
        (2, STENCIL_TAPS**2, 8, sea_width),
    )
    lanes = sea_width // LANES
    reached = (sea_rows + 2 * REACH, sea_cols + 2 * LEAD, sea_width)
    first = call(
        first_ocean_kernel,
        reached,
        edges,
        broad,
        north,
        south,
        kernels[0],
        ocean_gain[:1],
        ocean_up[0],
        ocean_down[0],
        scratch=[
            pltpu.VMEM((lanes, 3 * sea_rows, sea_cols + 2 * HALO, LANES), jnp.float32),
            pltpu.VMEM((lanes, 2, reached[1], LANES), jnp.float32),
        ],
        scalars=1,
    )
    returned, first = lax.optimization_barrier((returned, first))
    spatial = waves(
        (lon_count, lats, lon_dev, width), inverse, returned, lax.ppermute(returned, "comp", swap)
    )
    spatial, first = lax.optimization_barrier((spatial, first))
    spectral = lax.all_to_all(spatial, "lon", 0, 0, tiled=True).reshape(lat_dev, lon_dev, width)
    current = call(
        second_ocean_kernel,
        (sea_rows, sea_cols, sea_width),
        first,
        kernels[1],
        ocean_gain[1:],
        ocean_up[1],
        ocean_down[1],
        scratch=[
            pltpu.VMEM((lanes, *reached[:2], LANES), jnp.float32),
            pltpu.VMEM((lanes, 2, sea_cols, LANES), jnp.float32),
        ],
    )
    ocean_out = jnp.where(wet_mask[:, :, None] == 1, current, ocean_state)
    spectral, ocean_out = lax.optimization_barrier((spectral, ocean_out))
    atm_out = by_rows(
        epilogue_kernel,
        atm_state,
        flux_here,
        spectral,
        (surface_to_atm, atm_gain[1:], atm_up, atm_down),
    )
    return (atm_out, ocean_out)


def solution(mesh):
    placed = (
        P("lat", LON_COMP, None),
        P(("lat", "comp"), LON, None),
        P(("lat", "comp"), LON),
        P(("lat", "lon", "comp"), None, None),
        P(),
        P(),
        P(),
        P(),
        P(),
        P(),
        P(),
        P(),
        P(),
        P(),
        P(),
        P(),
        P(),
        P(),
        P(),
    )
    return jax.shard_map(
        local,
        mesh=mesh,
        in_specs=placed,
        out_specs=(P("lat", LON_COMP, None), P(("lat", "comp"), LON, None)),
        check_vma=False,
    )
```

```python
import math

import jax
import jax.numpy as jnp
import ml_dtypes
import numpy as np
from jax import lax
from jax.experimental import pallas as pl
from jax.experimental.pallas import tpu as pltpu
from jax.sharding import Mesh
from jax.sharding import PartitionSpec as P

MODES = 512
STENCIL_TAPS = 7
OCEAN_DILATION = 2
LAT = ("y", "z_hi")
LON = ("z_lo", "x")
ALL = (*LAT, *LON, "comp")
OWNERS = ("z_hi", "z_lo", "x", "y")


epsilon = 1e-05


def owner_order():
    count = lax.axis_size(LAT) * lax.axis_size(LON)
    return np.arange(count).reshape(lax.axis_size("y"), -1).T.reshape(-1)


def wave_tables(owners, lon_count, circle, owned):
    rows = (owners[:, None] * owned + np.arange(owned)).reshape(-1)
    block = circle // (2 * lon_count)
    where = np.arange(lon_count * block)
    forward, inverse = [], []
    row_sets = [rows // owned * 2 * owned + q * owned + rows % owned for q in range(2)]
    place_sets = [(where // block * 2 + q) * block + where % block for q in range(2)]

    def waves(row, place):
        phase = (row[:, None] // 2) * place[None, :] % circle
        angle = phase.astype(np.float32) * np.float32(2.0 * math.pi / circle)
        return np.where((row % 2 == 0)[:, None], np.cos(angle), -np.sin(angle)).astype(np.float32)

    for own in range(2):
        order = (own, 1 - own)
        f = np.concatenate([waves(row_sets[own], place_sets[q]) for q in order], 1)
        forward.append(f / np.float32(math.sqrt(circle)))
        g = []
        for q in order:
            factor = np.where(row_sets[q] // 2 == 0, 1.0, 2.0).astype(np.float32)
            g.append((waves(row_sets[q], place_sets[own]) * factor[:, None]).T)
        inverse.append(np.concatenate(g, 1) / np.float32(math.sqrt(circle)))
    return (
        np.stack(forward).astype(ml_dtypes.bfloat16),
        np.stack(inverse).astype(ml_dtypes.bfloat16),
    )


def waves_kernel(
    table_hbm, own_hbm, other_hbm, out_hbm, table_ref, own_ref, other_ref, held, sems
):
    lats, width = own_ref.shape[0], own_ref.shape[3]
    half = table_ref.shape[1] // 2
    table = pltpu.make_async_copy(table_hbm, table_ref, sems.at[0])
    table.start()
    owns, others, sends = [], [], []
    for i in range(lats):
        owns.append(pltpu.make_async_copy(own_hbm.at[:, i], own_ref.at[i], sems.at[1 + i]))
        owns[-1].start()
        at = sems.at[1 + lats + i]
        others.append(pltpu.make_async_copy(other_hbm.at[:, i], other_ref.at[i], at))
        others[-1].start()
    table.wait()
    for i in range(lats):
        owns[i].wait()
        total = jnp.dot(
            table_ref[:, :half],
            own_ref[i].reshape(half, width),
            preferred_element_type=jnp.float32,
        )
        others[i].wait()
        total += jnp.dot(
            table_ref[:, half:],
            other_ref[i].reshape(half, width),
            preferred_element_type=jnp.float32,
        )
        held[i] = total.astype(jnp.bfloat16).reshape(held.shape[1:])
        at = sems.at[1 + 2 * lats + i]
        sends.append(pltpu.make_async_copy(held.at[i], out_hbm.at[:, i], at))
        sends[-1].start()
    for send in sends:
        send.wait()


def waves(shape, table, own, other):
    lats = shape[1]
    return call(
        waves_kernel,
        shape,
        table,
        own,
        other,
        scratch=[
            pltpu.VMEM(table.shape, jnp.bfloat16),
            pltpu.VMEM((lats, own.shape[0], *own.shape[2:]), jnp.bfloat16),
            pltpu.VMEM((lats, own.shape[0], *own.shape[2:]), jnp.bfloat16),
            pltpu.VMEM((lats, shape[0], *shape[2:]), jnp.bfloat16),
            pltpu.SemaphoreType.DMA((1 + 3 * lats,)),
        ],
        behind=3,
        away=True,
    )


def filter_kernel(
    gain_ref,
    spectrum_hbm,
    weights_hbm,
    out_hbm,
    spectrum_ref,
    weighted_ref,
    mix_ref,
    turned_ref,
    rows_ref,
    held,
    sems,
):
    count = weighted_ref.shape[0]
    lats, owned, width = spectrum_ref.shape
    block = 64
    side = block * owned
    parts = lats // block
    targets = [weighted_ref.at[m] for m in range(count)]
    targets += [mix_ref.at[:, h * width : (h + 1) * width] for h in range(2)]
    targets += [turned_ref.at[m] for m in range(count)]
    arrivals = []
    for b in range(parts):
        part = pl.ds(b * block, block)
        at = sems.at[len(targets) + b]
        arrivals.append(pltpu.make_async_copy(spectrum_hbm.at[part], spectrum_ref.at[part], at))
        arrivals[-1].start()
    fetches, at = [], 0
    for n, target in enumerate(targets):
        size = target.shape[0]
        fetches.append(
            pltpu.make_async_copy(weights_hbm.at[pl.ds(at, size)], target, sems.at[n])
        )
        fetches[-1].start()
        at += size
    r = lax.broadcasted_iota(jnp.int32, (side, side), 0)
    s = lax.broadcasted_iota(jnp.int32, (side, side), 1)
    pick = jnp.where((r % block) * owned + r // block == s, 1.0, 0.0).astype(jnp.bfloat16)
    back = jnp.where((s % block) * owned + s // block == r, 1.0, 0.0).astype(jnp.bfloat16)

    def columns(p):
        return slice(p % 2 * width, (p % 2 + 1) * width)

    for b in range(parts):
        span = slice(b * block, (b + 1) * block)
        arrivals[b].wait()
        piece = spectrum_ref[span].reshape(side, width)
        moved = jnp.dot(pick, piece, preferred_element_type=jnp.float32).astype(jnp.bfloat16)
        for p in range(owned):
            rows_ref[p // 2, span, columns(p)] = moved[p * block : (p + 1) * block]
    gain = jnp.transpose(jnp.broadcast_to(gain_ref[...], (8, lats)))[:, :1]
    for fetch in fetches:
        fetch.wait()
    for m in range(count):
        coeffs = jnp.dot(weighted_ref[m], rows_ref[m], preferred_element_type=jnp.float32)
        mixed = jnp.dot(
            coeffs.astype(jnp.bfloat16), mix_ref[...], preferred_element_type=jnp.float32
        )
        filtered = (mixed * gain).astype(jnp.bfloat16)
        rows_ref[m] = jnp.dot(
            turned_ref[m], filtered, preferred_element_type=jnp.float32
        ).astype(jnp.bfloat16)
    sends = []
    for b in range(parts):
        span = slice(b * block, (b + 1) * block)
        piece = jnp.concatenate(
            [rows_ref[p // 2, span, columns(p)] for p in range(owned)], axis=0
        )
        moved = jnp.dot(back, piece, preferred_element_type=jnp.float32).astype(jnp.bfloat16)
        held[span] = moved.reshape(block, owned, width)
        at = sems.at[len(targets) + parts + b]
        part = pl.ds(b * block, block)
        sends.append(pltpu.make_async_copy(held.at[part], out_hbm.at[part], at))
        sends[-1].start()
    for send in sends:
        send.wait()


VMEM = 62_900_000


def call(kernel, shape, *args, scratch=(), room=0, scalars=0, behind=0, away=False):
    spaces = [pltpu.SMEM] * scalars + [pltpu.VMEM] * (len(args) - scalars - behind)
    spaces += [pltpu.HBM] * behind
    return pl.pallas_call(
        kernel,
        out_shape=jax.ShapeDtypeStruct(shape, jnp.bfloat16),
        in_specs=[pl.BlockSpec(memory_space=space) for space in spaces],
        out_specs=pl.BlockSpec(memory_space=pltpu.HBM if away else pltpu.VMEM),
        scratch_shapes=list(scratch),
        compiler_params=pltpu.CompilerParams(vmem_limit_bytes=VMEM - room),
    )(*args)


def gelu(x):
    inner = x * (math.sqrt(2.0 / math.pi) + (math.sqrt(2.0 / math.pi) * 0.044715) * (x * x))
    half = 0.5 * x
    return half + half * jnp.tanh(inner)


def normalised(values, gain):
    centred = values - jnp.mean(values, axis=-1, keepdims=True)
    spread = jnp.mean(centred * centred, axis=-1, keepdims=True)
    return (centred * lax.rsqrt(spread + epsilon) * gain).astype(jnp.bfloat16)


def prologue_kernel(atm_ref, flux_ref, out_weight_ref, gain_ref, out_hbm, held, sems):
    rows, lon_dev, width = atm_ref.shape
    each = rows // sems.shape[0]
    sends = []
    for k in range(sems.shape[0]):
        part = pl.ds(k * each, each)
        flux = flux_ref[pl.ds(k * each * lon_dev, each * lon_dev)]
        forced = atm_ref[part].reshape(each * lon_dev, width).astype(jnp.float32) + jnp.dot(
            flux, out_weight_ref[...], preferred_element_type=jnp.float32
        )
        held[part] = normalised(forced, gain_ref[...]).reshape(each, lon_dev, width)
        sends.append(pltpu.make_async_copy(held.at[part], out_hbm.at[part], sems.at[k]))
        sends[-1].start()
    for send in sends:
        send.wait()


def epilogue_kernel(
    atm_ref, flux_ref, spectral_ref, out_weight_ref, gain_ref, up_ref, down_ref, out_ref
):
    rows, lon_dev, width = atm_ref.shape
    each = rows // 2
    side = each * lon_dev
    for k in range(2):
        part = pl.ds(k * each, each)
        forced = atm_ref[part].reshape(side, width).astype(jnp.float32) + jnp.dot(
            flux_ref[pl.ds(k * side, side)],
            out_weight_ref[...],
            preferred_element_type=jnp.float32,
        )
        mixed = forced + spectral_ref[part].reshape(side, width).astype(jnp.float32)
        normed = normalised(mixed, gain_ref[...])
        hidden = gelu(jnp.dot(normed, up_ref[...], preferred_element_type=jnp.float32))
        total = mixed + jnp.dot(
            hidden.astype(jnp.bfloat16), down_ref[...], preferred_element_type=jnp.float32
        )
        out_ref[part] = total.astype(jnp.bfloat16).reshape(each, lon_dev, width)


def epilogue(atm, flux, spectral, *weights, rows=8):
    lat_dev, lon_dev, width = atm.shape
    field = pl.BlockSpec((rows, lon_dev, width), lambda i: (i, 0, 0))
    specs = [field, pl.BlockSpec((rows * lon_dev, flux.shape[1]), lambda i: (i, 0)), field]
    specs += [pl.BlockSpec(w.shape, lambda i: (0, 0)) for w in weights]
    return pl.pallas_call(
        epilogue_kernel,
        grid=(lat_dev // rows,),
        out_shape=jax.ShapeDtypeStruct(atm.shape, jnp.bfloat16),
        in_specs=specs,
        out_specs=field,
        compiler_params=pltpu.CompilerParams(vmem_limit_bytes=VMEM - 38000000),
    )(atm, flux, spectral, *weights)


HALO = 16
LEAD = 8
LANES = 128
REACH = STENCIL_TAPS // 2 * OCEAN_DILATION


def ocean_rows(field, kern, gain, up, down, sums, out_ref, group, low, high):
    blocks = field.shape[0]
    rows, cols, width = out_ref.shape
    stride = cols // 8
    each = stride // OCEAN_DILATION

    def step(g, carry):
        top = g * group
        for r in range(group):
            for lane in range(blocks):
                part = slice(lane * LANES, (lane + 1) * LANES)
                for parity in range(OCEAN_DILATION):
                    acc = [None] * each
                    for a in range(STENCIL_TAPS):
                        row = top + r + a * OCEAN_DILATION
                        first = LEAD - REACH + parity
                        loads = [
                            field[lane, row, pl.ds(first + OCEAN_DILATION * q, 8, stride=stride), :]
                            for q in range(each + STENCIL_TAPS - 1)
                        ]
                        for b in range(STENCIL_TAPS):
                            weight = kern[a * STENCIL_TAPS + b, :, part]
                            for q in range(each):
                                term = loads[q + b] * weight
                                acc[q] = term if acc[q] is None else acc[q] + term
                    for q in range(each):
                        at = pl.ds(parity + OCEAN_DILATION * q, 8, stride=stride)
                        sums[lane, r, at, :] = acc[q]
        side = group * cols
        stencil = jnp.concatenate(
            [sums[lane].reshape(side, LANES) for lane in range(blocks)], axis=1
        )
        normed = normalised(stencil, gain[...])
        hidden = gelu(jnp.dot(normed, up[...], preferred_element_type=jnp.float32))
        total = jnp.dot(
            hidden.astype(jnp.bfloat16), down[...], preferred_element_type=jnp.float32
        )
        for r in range(group):
            centre = jnp.concatenate(
                [field[lane, top + r + REACH, LEAD : LEAD + cols, :] for lane in range(blocks)],
                axis=1,
            )
            value = centre + total[r * cols : (r + 1) * cols]
            col = lax.broadcasted_iota(jnp.int32, value.shape, 0)
            value = jnp.where((col >= low) & (col < high), value, 0.0)
            out_ref[top + r] = value.astype(jnp.bfloat16)
        return carry

    lax.fori_loop(0, rows // group, step, 0)


def ocean_kernel(
    inside_ref,
    centre_ref,
    north_ref,
    south_ref,
    kern_ref,
    gain_ref,
    up_ref,
    down_ref,
    out_ref,
    field,
    sums,
):
    at = 0
    for ref in (north_ref, centre_ref, south_ref):
        for lane in range(field.shape[0]):
            field[lane, at : at + ref.shape[0]] = ref[
                :, :, lane * LANES : (lane + 1) * LANES
            ].astype(jnp.float32)
        at += ref.shape[0]
    group = sums.shape[1]
    low, high = inside_ref[0], inside_ref[1]
    ocean_rows(field, kern_ref, gain_ref, up_ref, down_ref, sums, out_ref, group, low, high)


def ocean_block(first_col, circle, centre, north, south, kern, gain, up, down):
    rows, cols, width = centre.shape
    blocks, out_cols = width // LANES, cols - 2 * LEAD
    return call(
        ocean_kernel,
        (rows, out_cols, width),
        jnp.stack([-first_col, circle - first_col]).astype(jnp.int32),
        centre,
        north,
        south,
        kern,
        gain,
        up,
        down,
        scratch=[
            pltpu.VMEM((blocks, rows + 2 * REACH, cols, LANES), jnp.float32),
            pltpu.VMEM((blocks, 4, out_cols, LANES), jnp.float32),
        ],
        scalars=1,
        room=38_000_000,
    )


def shifted(block, dy, dx):
    tall = lax.axis_size(LAT) * lax.axis_size("comp")
    broad = lax.axis_size(LON)

    def place(y, x):
        return (y // 2 * broad + x) * 2 + y % 2

    pairs = [
        (place(y, x), place(y + dy, x + dx))
        for y in range(tall)
        for x in range(broad)
        if 0 <= y + dy < tall and 0 <= x + dx < broad
    ]
    return lax.ppermute(block, ALL, pairs)


def local(
    atm_state,
    ocean_state,
    wet_mask,
    legendre,
    quad_weight,
    spec_real,
    spec_imag,
    degree_gain,
    atm_gain,
    atm_up,
    atm_down,
    atm_to_surface,
    surface_to_atm,
    ocean_to_surface,
    surface_to_ocean,
    ocean_kernel,
    ocean_gain,
    ocean_up,
    ocean_down,
):
    lat_count = lax.axis_size(LAT)
    lon_count = lax.axis_size(LON)
    lat_dev, lon_dev, width = atm_state.shape
    sea_rows, sea_cols, sea_width = ocean_state.shape
    lat_total = lat_dev * lat_count
    circle = lon_dev * lon_count * 2
    owned = 2 * legendre.shape[0]
    owners = lat_count * lon_count
    order = owner_order()
    lats = lat_dev // lon_count
    me = lax.axis_index("comp")
    swap = [(0, 1), (1, 0)]
    forward, inverse = wave_tables(order, lon_count, circle, owned)
    forward = lax.dynamic_index_in_dim(jnp.asarray(forward), me, 0, keepdims=False)
    inverse = lax.dynamic_index_in_dim(jnp.asarray(inverse), me, 0, keepdims=False)
    wet = wet_mask.astype(jnp.float32)[:, :, None]
    ocean_flux = (
        jnp.dot(ocean_state, ocean_to_surface, preferred_element_type=jnp.float32) * wet
    ).astype(jnp.bfloat16)
    atm_flux = jnp.dot(atm_state, atm_to_surface, preferred_element_type=jnp.float32).astype(
        jnp.bfloat16
    )

    def halves(mine, dim):
        low, high = jnp.split(mine, 2, axis=dim)
        return (jnp.where(me == 0, low, high), jnp.where(me == 0, high, low))

    def together(kept, got, dim):
        low = jnp.where(me == 0, kept, got)
        high = jnp.where(me == 0, got, kept)
        return jnp.concatenate([low, high], axis=dim)

    kept_ocean, sent_ocean = halves(ocean_flux, 1)
    kept_atm, sent_atm = halves(atm_flux, 0)
    got_ocean = lax.ppermute(sent_ocean, "comp", swap)
    flux_here = together(kept_ocean, got_ocean, 0).reshape(lat_dev * lon_dev, -1)
    normed = call(
        prologue_kernel,
        atm_state.shape,
        atm_state,
        flux_here,
        surface_to_atm,
        atm_gain[:1],
        scratch=[pltpu.VMEM(atm_state.shape, jnp.bfloat16), pltpu.SemaphoreType.DMA((3,))],
        away=True,
        room=24000000,
    )
    rings = lax.all_to_all(
        normed.reshape(lon_count, lats, lon_dev, width), LON, 0, 0, tiled=True
    )
    flux_sea = together(kept_atm, lax.ppermute(sent_atm, "comp", swap), 1)
    ocean_in = (
        ocean_state.astype(jnp.float32)
        + wet * jnp.dot(flux_sea, surface_to_ocean, preferred_element_type=jnp.float32)
    ).astype(jnp.bfloat16)
    west = shifted(ocean_in[:, -HALO:], 0, 1)
    east = shifted(ocean_in[:, :HALO], 0, -1)
    broad = jnp.concatenate([west, ocean_in, east], axis=1)
    rings, broad = lax.optimization_barrier((rings, broad))
    seen = (order[:, None] * lats + np.arange(lats)).reshape(-1)
    moved = jnp.asarray(np.eye(lat_total)[:, seen].astype(ml_dtypes.bfloat16))
    table = jnp.einsum(
        "mlt,ts->mls", legendre, moved, preferred_element_type=jnp.float32
    ).astype(jnp.bfloat16)
    weight = quad_weight.reshape(lax.axis_size("y"), -1, lats).swapaxes(0, 1).reshape(-1)
    weighted = (table.astype(jnp.float32) * (weight / lat_total)).astype(jnp.bfloat16)
    turned = jnp.swapaxes(table, 1, 2)
    spectrum = waves(
        (owners, lats, owned, width), forward, rings, lax.ppermute(rings, "comp", swap)
    )
    spectrum, broad = lax.optimization_barrier((spectrum, broad))
    gathered = lax.all_to_all(spectrum, OWNERS, 0, 0, tiled=True)
    north = shifted(broad[-REACH:], 1, 0)
    south = shifted(broad[:REACH], -1, 0)
    weights = jnp.concatenate(
        [*weighted, spec_real, -spec_imag, spec_imag, spec_real, *turned], axis=0
    )
    filtered = call(
        filter_kernel,
        (lat_total, owned, width),
        degree_gain[None],
        gathered.reshape(lat_total, owned, width),
        weights,
        scratch=[
            pltpu.VMEM((lat_total, owned, width), jnp.bfloat16),
            pltpu.VMEM(weighted.shape, jnp.bfloat16),
            pltpu.VMEM((2 * width, 2 * width), jnp.bfloat16),
            pltpu.VMEM(turned.shape, jnp.bfloat16),
            pltpu.VMEM((owned // 2, lat_total, 2 * width), jnp.bfloat16),
            pltpu.VMEM((lat_total, owned, width), jnp.bfloat16),
            pltpu.SemaphoreType.DMA((6 + lat_total // 64 * 2,)),
        ],
        behind=2,
        away=True,
        room=100000,
    )
    filtered, broad, north, south = lax.optimization_barrier((filtered, broad, north, south))
    returned = lax.all_to_all(
        filtered.reshape(owners, lats, owned, width), OWNERS, 0, 0, tiled=True
    )
    first_col = lax.axis_index(LON) * sea_cols
    kernels = jnp.broadcast_to(
        ocean_kernel.astype(jnp.float32).reshape(2, STENCIL_TAPS**2, 1, sea_width),
        (2, STENCIL_TAPS**2, 8, sea_width),
    )
    blocks = [
        (kernels[k], ocean_gain[k : k + 1], ocean_up[k], ocean_down[k]) for k in range(2)
    ]
    first = ocean_block(first_col - LEAD, circle, broad, north, south, *blocks[0])
    returned, first = lax.optimization_barrier((returned, first))
    spatial = waves(
        (lon_count, lats, lon_dev, width), inverse, returned, lax.ppermute(returned, "comp", swap)
    )
    north = shifted(first[-REACH:], 1, 0)
    south = shifted(first[:REACH], -1, 0)
    spatial, first, north, south = lax.optimization_barrier((spatial, first, north, south))
    spectral = lax.all_to_all(spatial, LON, 0, 0, tiled=True).reshape(lat_dev, lon_dev, width)
    current = ocean_block(first_col, circle, first, north, south, *blocks[1])
    ocean_out = jnp.where(wet_mask[:, :, None] == 1, current, ocean_state)
    spectral, ocean_out = lax.optimization_barrier((spectral, ocean_out))
    atm_out = epilogue(
        atm_state, flux_here, spectral, surface_to_atm, atm_gain[1:], atm_up, atm_down
    )
    return (atm_out, ocean_out)


def solution(mesh):
    lat_count, lon_count = mesh.shape["lat"], mesh.shape["lon"]
    torus = Mesh(
        mesh.devices.reshape(4, lat_count // 4, lon_count // 4, 4, mesh.shape["comp"]), ALL
    )
    atm, sea = P(LAT, (*LON, "comp"), None), P((*LAT, "comp"), LON, None)
    placed = (atm, sea, P((*LAT, "comp"), LON), P(ALL, None, None)) + (P(),) * 15
    return jax.shard_map(
        local, mesh=torus, in_specs=placed, out_specs=(atm, sea), check_vma=False
    )
```

```python
import functools
import math

import jax
import jax.numpy as jnp
import ml_dtypes
import numpy as np
from jax import lax
from jax.experimental import pallas as pl
from jax.experimental.pallas import tpu as pltpu
from jax.sharding import Mesh
from jax.sharding import PartitionSpec as P

MODES = 512
STENCIL_TAPS = 7
OCEAN_DILATION = 2
LAT = ("y", "z_hi")
LON = ("z_lo", "x")
ALL = (*LAT, *LON, "comp")
OWNERS = ("z_hi", "z_lo", "x", "y")


epsilon = 1e-05


def owner_order():
    count = lax.axis_size(LAT) * lax.axis_size(LON)
    return np.arange(count).reshape(lax.axis_size("y"), -1).T.reshape(-1)


def wave_tables(owners, lon_count, circle, owned):
    rows = (owners[:, None] * owned + np.arange(owned)).reshape(-1)
    block = circle // (2 * lon_count)
    where = np.arange(lon_count * block)
    forward, inverse = [], []
    row_sets = [rows // owned * 2 * owned + q * owned + rows % owned for q in range(2)]
    place_sets = [(where // block * 2 + q) * block + where % block for q in range(2)]

    def waves(row, place):
        phase = (row[:, None] // 2) * place[None, :] % circle
        angle = phase.astype(np.float32) * np.float32(2.0 * math.pi / circle)
        return np.where((row % 2 == 0)[:, None], np.cos(angle), -np.sin(angle)).astype(np.float32)

    for own in range(2):
        order = (own, 1 - own)
        f = np.concatenate([waves(row_sets[own], place_sets[q]) for q in order], 1)
        forward.append(f / np.float32(math.sqrt(circle)))
        g = []
        for q in order:
            factor = np.where(row_sets[q] // 2 == 0, 1.0, 2.0).astype(np.float32)
            g.append((waves(row_sets[q], place_sets[own]) * factor[:, None]).T)
        inverse.append(np.concatenate(g, 1) / np.float32(math.sqrt(circle)))
    return (
        np.stack(forward).astype(ml_dtypes.bfloat16),
        np.stack(inverse).astype(ml_dtypes.bfloat16),
    )


def waves_kernel(
    table_hbm, own_hbm, other_hbm, out_hbm, table_ref, own_ref, other_ref, held, sems
):
    lats, width = own_ref.shape[0], own_ref.shape[3]
    half = table_ref.shape[1] // 2
    table = pltpu.make_async_copy(table_hbm, table_ref, sems.at[0])
    table.start()
    owns, others, sends = [], [], []
    for i in range(lats):
        owns.append(pltpu.make_async_copy(own_hbm.at[:, i], own_ref.at[i], sems.at[1 + i]))
        owns[-1].start()
        at = sems.at[1 + lats + i]
        others.append(pltpu.make_async_copy(other_hbm.at[:, i], other_ref.at[i], at))
        others[-1].start()
    table.wait()
    for i in range(lats):
        owns[i].wait()
        total = jnp.dot(
            table_ref[:, :half],
            own_ref[i].reshape(half, width),
            preferred_element_type=jnp.float32,
        )
        others[i].wait()
        total += jnp.dot(
            table_ref[:, half:],
            other_ref[i].reshape(half, width),
            preferred_element_type=jnp.float32,
        )
        held[i] = total.astype(jnp.bfloat16).reshape(held.shape[1:])
        at = sems.at[1 + 2 * lats + i]
        sends.append(pltpu.make_async_copy(held.at[i], out_hbm.at[:, i], at))
        sends[-1].start()
    for send in sends:
        send.wait()


def waves(shape, table, own, other):
    lats = shape[1]
    return call(
        waves_kernel,
        shape,
        table,
        own,
        other,
        scratch=[
            pltpu.VMEM(table.shape, jnp.bfloat16),
            pltpu.VMEM((lats, own.shape[0], *own.shape[2:]), jnp.bfloat16),
            pltpu.VMEM((lats, own.shape[0], *own.shape[2:]), jnp.bfloat16),
            pltpu.VMEM((lats, shape[0], *shape[2:]), jnp.bfloat16),
            pltpu.SemaphoreType.DMA((1 + 3 * lats,)),
        ],
        behind=3,
        away=True,
    )


def filter_kernel(
    gain_ref,
    spectrum_hbm,
    weights_hbm,
    out_hbm,
    spectrum_ref,
    weighted_ref,
    mix_ref,
    turned_ref,
    rows_ref,
    held,
    sems,
):
    count = weighted_ref.shape[0]
    lats, owned, width = spectrum_ref.shape
    block = 64
    side = block * owned
    parts = lats // block
    targets = [weighted_ref.at[m] for m in range(count)]
    targets += [mix_ref.at[:, h * width : (h + 1) * width] for h in range(2)]
    targets += [turned_ref.at[m] for m in range(count)]
    arrivals = []
    for b in range(parts):
        part = pl.ds(b * block, block)
        at = sems.at[len(targets) + b]
        arrivals.append(pltpu.make_async_copy(spectrum_hbm.at[part], spectrum_ref.at[part], at))
        arrivals[-1].start()
    fetches, at = [], 0
    for n, target in enumerate(targets):
        size = target.shape[0]
        fetches.append(
            pltpu.make_async_copy(weights_hbm.at[pl.ds(at, size)], target, sems.at[n])
        )
        fetches[-1].start()
        at += size
    r = lax.broadcasted_iota(jnp.int32, (side, side), 0)
    s = lax.broadcasted_iota(jnp.int32, (side, side), 1)
    pick = jnp.where((r % block) * owned + r // block == s, 1.0, 0.0).astype(jnp.bfloat16)
    back = jnp.where((s % block) * owned + s // block == r, 1.0, 0.0).astype(jnp.bfloat16)

    def columns(p):
        return slice(p % 2 * width, (p % 2 + 1) * width)

    for b in range(parts):
        span = slice(b * block, (b + 1) * block)
        arrivals[b].wait()
        piece = spectrum_ref[span].reshape(side, width)
        moved = jnp.dot(pick, piece, preferred_element_type=jnp.float32).astype(jnp.bfloat16)
        for p in range(owned):
            rows_ref[p // 2, span, columns(p)] = moved[p * block : (p + 1) * block]
    gain = jnp.transpose(jnp.broadcast_to(gain_ref[...], (8, lats)))[:, :1]
    for fetch in fetches:
        fetch.wait()
    for m in range(count):
        coeffs = jnp.dot(weighted_ref[m], rows_ref[m], preferred_element_type=jnp.float32)
        mixed = jnp.dot(
            coeffs.astype(jnp.bfloat16), mix_ref[...], preferred_element_type=jnp.float32
        )
        filtered = (mixed * gain).astype(jnp.bfloat16)
        rows_ref[m] = jnp.dot(
            turned_ref[m], filtered, preferred_element_type=jnp.float32
        ).astype(jnp.bfloat16)
    sends = []
    for b in range(parts):
        span = slice(b * block, (b + 1) * block)
        piece = jnp.concatenate(
            [rows_ref[p // 2, span, columns(p)] for p in range(owned)], axis=0
        )
        moved = jnp.dot(back, piece, preferred_element_type=jnp.float32).astype(jnp.bfloat16)
        held[span] = moved.reshape(block, owned, width)
        at = sems.at[len(targets) + parts + b]
        part = pl.ds(b * block, block)
        sends.append(pltpu.make_async_copy(held.at[part], out_hbm.at[part], at))
        sends[-1].start()
    for send in sends:
        send.wait()


VMEM = 62_900_000


def call(kernel, shape, *args, scratch=(), room=0, scalars=0, behind=0, away=False):
    spaces = [pltpu.SMEM] * scalars + [pltpu.VMEM] * (len(args) - scalars - behind)
    spaces += [pltpu.HBM] * behind
    return pl.pallas_call(
        kernel,
        out_shape=jax.ShapeDtypeStruct(shape, jnp.bfloat16),
        in_specs=[pl.BlockSpec(memory_space=space) for space in spaces],
        out_specs=pl.BlockSpec(memory_space=pltpu.HBM if away else pltpu.VMEM),
        scratch_shapes=list(scratch),
        compiler_params=pltpu.CompilerParams(vmem_limit_bytes=VMEM - room),
    )(*args)


def gelu(x):
    inner = x * (math.sqrt(2.0 / math.pi) + (math.sqrt(2.0 / math.pi) * 0.044715) * (x * x))
    half = 0.5 * x
    return half + half * jnp.tanh(inner)


def normalised(values, gain):
    centred = values - jnp.mean(values, axis=-1, keepdims=True)
    spread = jnp.mean(centred * centred, axis=-1, keepdims=True)
    return (centred * lax.rsqrt(spread + epsilon) * gain).astype(jnp.bfloat16)


def prologue_kernel(atm_ref, flux_ref, out_weight_ref, gain_ref, out_hbm, held, sems):
    rows, lon_dev, width = atm_ref.shape
    each = rows // sems.shape[0]
    sends = []
    for k in range(sems.shape[0]):
        part = pl.ds(k * each, each)
        flux = flux_ref[pl.ds(k * each * lon_dev, each * lon_dev)]
        forced = atm_ref[part].reshape(each * lon_dev, width).astype(jnp.float32) + jnp.dot(
            flux, out_weight_ref[...], preferred_element_type=jnp.float32
        )
        held[part] = normalised(forced, gain_ref[...]).reshape(each, lon_dev, width)
        sends.append(pltpu.make_async_copy(held.at[part], out_hbm.at[part], sems.at[k]))
        sends[-1].start()
    for send in sends:
        send.wait()


def epilogue_kernel(
    gain_ref,
    out_weight_ref,
    flux_ref,
    atm_hbm,
    spectral_hbm,
    up_hbm,
    down_hbm,
    out_hbm,
    atm,
    spectral,
    up,
    down,
    held,
    sems,
):
    rows, lon_dev, width = atm.shape
    parts = 3
    each = rows // parts
    side = each * lon_dev
    spans = [pl.ds(k * each, each) for k in range(parts)]
    fields = [
        [
            pltpu.make_async_copy(atm_hbm.at[span], atm.at[span], sems.at[k]),
            pltpu.make_async_copy(spectral_hbm.at[span], spectral.at[span], sems.at[parts + k]),
        ]
        for k, span in enumerate(spans)
    ]
    weights = [
        pltpu.make_async_copy(up_hbm, up, sems.at[3 * parts]),
        pltpu.make_async_copy(down_hbm, down, sems.at[3 * parts + 1]),
    ]
    for copy in fields[0] + weights + [c for pair in fields[1:] for c in pair]:
        copy.start()
    sends = []
    for k, span in enumerate(spans):
        for copy in fields[k]:
            copy.wait()
        forced = atm[span].reshape(side, width).astype(jnp.float32) + jnp.dot(
            flux_ref[pl.ds(k * side, side)],
            out_weight_ref[...],
            preferred_element_type=jnp.float32,
        )
        mixed = forced + spectral[span].reshape(side, width).astype(jnp.float32)
        normed = normalised(mixed, gain_ref[...])
        if k == 0:
            weights[0].wait()
        hidden = gelu(jnp.dot(normed, up[...], preferred_element_type=jnp.float32))
        if k == 0:
            weights[1].wait()
        total = mixed + jnp.dot(
            hidden.astype(jnp.bfloat16), down[...], preferred_element_type=jnp.float32
        )
        held[span] = total.astype(jnp.bfloat16).reshape(each, lon_dev, width)
        sends.append(
            pltpu.make_async_copy(held.at[span], out_hbm.at[span], sems.at[2 * parts + k])
        )
        sends[-1].start()
    for send in sends:
        send.wait()


def epilogue(atm, flux, spectral, out_weight, gain, up, down):
    return call(
        epilogue_kernel,
        atm.shape,
        gain,
        out_weight,
        flux,
        atm,
        spectral,
        up,
        down,
        scratch=[
            pltpu.VMEM(atm.shape, jnp.bfloat16),
            pltpu.VMEM(atm.shape, jnp.bfloat16),
            pltpu.VMEM(up.shape, jnp.bfloat16),
            pltpu.VMEM(down.shape, jnp.bfloat16),
            pltpu.VMEM(atm.shape, jnp.bfloat16),
            pltpu.SemaphoreType.DMA((11,)),
        ],
        behind=4,
        away=True,
        room=100_000,
    )


HALO = 16
LEAD = 8
LANES = 128
REACH = STENCIL_TAPS // 2 * OCEAN_DILATION


def ocean_kernel(
    inside_ref,
    gain_ref,
    north_hbm,
    upper_hbm,
    lower_hbm,
    south_hbm,
    kern_hbm,
    up_hbm,
    down_hbm,
    *rest,
    block,
    group,
):
    *outs, staged, field, kern, up, down, sums, held, sems = rest
    half = staged.shape[1]
    blocks = field.shape[0]
    rows, cols, width = held.shape
    stride = cols // 8
    each = stride // OCEAN_DILATION
    arrivals = [pltpu.make_async_copy(kern_hbm.at[block], kern, sems.at[0])]
    for n, piece in enumerate((north_hbm, upper_hbm, lower_hbm, south_hbm)):
        arrivals.append(pltpu.make_async_copy(piece, staged.at[n], sems.at[1 + n]))
    weights = [
        pltpu.make_async_copy(up_hbm.at[block], up, sems.at[5]),
        pltpu.make_async_copy(down_hbm.at[block], down, sems.at[6]),
    ]
    for copy in arrivals + weights:
        copy.start()
    for n in range(4):
        arrivals[1 + n].wait()
        for lane in range(blocks):
            field[lane, n * half : (n + 1) * half] = staged[
                n, :, :, lane * LANES : (lane + 1) * LANES
            ].astype(jnp.float32)
    arrivals[0].wait()
    low, high = inside_ref[0], inside_ref[1]

    def stencil(top):
        for r in range(group):
            for lane in range(blocks):
                part = slice(lane * LANES, (lane + 1) * LANES)
                for parity in range(OCEAN_DILATION):
                    acc = [None] * each
                    for a in range(STENCIL_TAPS):
                        row = top + r + a * OCEAN_DILATION
                        first = LEAD - REACH + parity
                        loads = [
                            field[lane, row, pl.ds(first + OCEAN_DILATION * q, 8, stride=stride), :]
                            for q in range(each + STENCIL_TAPS - 1)
                        ]
                        for b in range(STENCIL_TAPS):
                            weight = kern[a * STENCIL_TAPS + b, :, part]
                            for q in range(each):
                                term = loads[q + b] * weight
                                acc[q] = term if acc[q] is None else acc[q] + term
                    for q in range(each):
                        at = pl.ds(parity + OCEAN_DILATION * q, 8, stride=stride)
                        sums[lane, r, at, :] = acc[q]

    def layers(top):
        side = group * cols
        joined = jnp.concatenate(
            [sums[lane].reshape(side, LANES) for lane in range(blocks)], axis=1
        )
        normed = normalised(joined, gain_ref[...])
        hidden = gelu(jnp.dot(normed, up[...], preferred_element_type=jnp.float32))
        total = jnp.dot(
            hidden.astype(jnp.bfloat16), down[...], preferred_element_type=jnp.float32
        )
        for r in range(group):
            centre = jnp.concatenate(
                [field[lane, top + r + REACH, LEAD : LEAD + cols, :] for lane in range(blocks)],
                axis=1,
            )
            value = centre + total[r * cols : (r + 1) * cols]
            col = lax.broadcasted_iota(jnp.int32, value.shape, 0)
            value = jnp.where((col >= low) & (col < high), value, 0.0)
            held[top + r] = value.astype(jnp.bfloat16)

    def step(g, carry):
        stencil(g * group)

        @pl.when(g == 0)
        def _():
            for copy in weights:
                copy.wait()

        layers(g * group)
        return carry

    lax.fori_loop(0, rows // group, step, 0)
    sends = []
    each_out = rows // len(outs)
    for n, out in enumerate(outs):
        part = pl.ds(n * each_out, each_out)
        sends.append(pltpu.make_async_copy(held.at[part], out, sems.at[7 + n]))
        sends[-1].start()
    for send in sends:
        send.wait()


def ocean_block(first_col, circle, pieces, kern, gain, up, down, block, parts):
    half, cols, width = pieces[0].shape
    blocks, out_cols, rows = width // LANES, cols - 2 * LEAD, 2 * half
    group = 4
    out = jax.ShapeDtypeStruct((rows // parts, out_cols, width), jnp.bfloat16)
    hbm = pl.BlockSpec(memory_space=pltpu.HBM)
    return pl.pallas_call(
        functools.partial(ocean_kernel, block=block, group=group),
        out_shape=[out] * parts,
        in_specs=[
            pl.BlockSpec(memory_space=pltpu.SMEM),
            pl.BlockSpec(memory_space=pltpu.VMEM),
            *[hbm] * 7,
        ],
        out_specs=[hbm] * parts,
        scratch_shapes=[
            pltpu.VMEM((4, half, cols, width), jnp.bfloat16),
            pltpu.VMEM((blocks, 4 * half, cols, LANES), jnp.float32),
            pltpu.VMEM(kern.shape[1:], jnp.float32),
            pltpu.VMEM(up.shape[1:], jnp.bfloat16),
            pltpu.VMEM(down.shape[1:], jnp.bfloat16),
            pltpu.VMEM((blocks, group, out_cols, LANES), jnp.float32),
            pltpu.VMEM((rows, out_cols, width), jnp.bfloat16),
            pltpu.SemaphoreType.DMA((7 + parts,)),
        ],
        compiler_params=pltpu.CompilerParams(vmem_limit_bytes=VMEM - 100_000),
    )(
        jnp.stack([-first_col, circle - first_col]).astype(jnp.int32),
        gain[block : block + 1],
        *pieces,
        kern,
        up,
        down,
    )


def shifted(block, dy, dx):
    tall = lax.axis_size(LAT) * lax.axis_size("comp")
    broad = lax.axis_size(LON)

    def place(y, x):
        return (y // 2 * broad + x) * 2 + y % 2

    pairs = [
        (place(y, x), place(y + dy, x + dx))
        for y in range(tall)
        for x in range(broad)
        if 0 <= y + dy < tall and 0 <= x + dx < broad
    ]
    return lax.ppermute(block, ALL, pairs)


def local(
    atm_state,
    ocean_state,
    wet_mask,
    legendre,
    quad_weight,
    spec_real,
    spec_imag,
    degree_gain,
    atm_gain,
    atm_up,
    atm_down,
    atm_to_surface,
    surface_to_atm,
    ocean_to_surface,
    surface_to_ocean,
    ocean_kernel,
    ocean_gain,
    ocean_up,
    ocean_down,
):
    lat_count = lax.axis_size(LAT)
    lon_count = lax.axis_size(LON)
    lat_dev, lon_dev, width = atm_state.shape
    sea_rows, sea_cols, sea_width = ocean_state.shape
    lat_total = lat_dev * lat_count
    circle = lon_dev * lon_count * 2
    owned = 2 * legendre.shape[0]
    owners = lat_count * lon_count
    order = owner_order()
    lats = lat_dev // lon_count
    me = lax.axis_index("comp")
    swap = [(0, 1), (1, 0)]
    forward, inverse = wave_tables(order, lon_count, circle, owned)
    forward = lax.dynamic_index_in_dim(jnp.asarray(forward), me, 0, keepdims=False)
    inverse = lax.dynamic_index_in_dim(jnp.asarray(inverse), me, 0, keepdims=False)
    wet = wet_mask.astype(jnp.float32)[:, :, None]
    ocean_flux = (
        jnp.dot(ocean_state, ocean_to_surface, preferred_element_type=jnp.float32) * wet
    ).astype(jnp.bfloat16)
    atm_flux = jnp.dot(atm_state, atm_to_surface, preferred_element_type=jnp.float32).astype(
        jnp.bfloat16
    )

    def halves(mine, dim):
        low, high = jnp.split(mine, 2, axis=dim)
        return (jnp.where(me == 0, low, high), jnp.where(me == 0, high, low))

    def together(kept, got, dim):
        low = jnp.where(me == 0, kept, got)
        high = jnp.where(me == 0, got, kept)
        return jnp.concatenate([low, high], axis=dim)

    kept_ocean, sent_ocean = halves(ocean_flux, 1)
    kept_atm, sent_atm = halves(atm_flux, 0)
    got_ocean = lax.ppermute(sent_ocean, "comp", swap)
    flux_here = together(kept_ocean, got_ocean, 0).reshape(lat_dev * lon_dev, -1)
    normed = call(
        prologue_kernel,
        atm_state.shape,
        atm_state,
        flux_here,
        surface_to_atm,
        atm_gain[:1],
        scratch=[pltpu.VMEM(atm_state.shape, jnp.bfloat16), pltpu.SemaphoreType.DMA((3,))],
        away=True,
        room=24000000,
    )
    rings = lax.all_to_all(
        normed.reshape(lon_count, lats, lon_dev, width), LON, 0, 0, tiled=True
    )
    flux_sea = together(kept_atm, lax.ppermute(sent_atm, "comp", swap), 1)
    ocean_in = (
        ocean_state.astype(jnp.float32)
        + wet * jnp.dot(flux_sea, surface_to_ocean, preferred_element_type=jnp.float32)
    ).astype(jnp.bfloat16)
    west = shifted(ocean_in[:, -HALO:], 0, 1)
    east = shifted(ocean_in[:, :HALO], 0, -1)
    upper, lower = [
        jnp.concatenate([west[part], ocean_in[part], east[part]], axis=1)
        for part in (slice(0, REACH), slice(REACH, None))
    ]
    rings, upper, lower = lax.optimization_barrier((rings, upper, lower))
    seen = (order[:, None] * lats + np.arange(lats)).reshape(-1)
    moved = jnp.asarray(np.eye(lat_total)[:, seen].astype(ml_dtypes.bfloat16))
    table = jnp.einsum(
        "mlt,ts->mls", legendre, moved, preferred_element_type=jnp.float32
    ).astype(jnp.bfloat16)
    weight = quad_weight.reshape(lax.axis_size("y"), -1, lats).swapaxes(0, 1).reshape(-1)
    weighted = (table.astype(jnp.float32) * (weight / lat_total)).astype(jnp.bfloat16)
    turned = jnp.swapaxes(table, 1, 2)
    spectrum = waves(
        (owners, lats, owned, width), forward, rings, lax.ppermute(rings, "comp", swap)
    )
    spectrum, upper, lower = lax.optimization_barrier((spectrum, upper, lower))
    gathered = lax.all_to_all(spectrum, OWNERS, 0, 0, tiled=True)
    north, south = shifted(lower, 1, 0), shifted(upper, -1, 0)
    weights = jnp.concatenate(
        [*weighted, spec_real, -spec_imag, spec_imag, spec_real, *turned], axis=0
    )
    filtered = call(
        filter_kernel,
        (lat_total, owned, width),
        degree_gain[None],
        gathered.reshape(lat_total, owned, width),
        weights,
        scratch=[
            pltpu.VMEM((lat_total, owned, width), jnp.bfloat16),
            pltpu.VMEM(weighted.shape, jnp.bfloat16),
            pltpu.VMEM((2 * width, 2 * width), jnp.bfloat16),
            pltpu.VMEM(turned.shape, jnp.bfloat16),
            pltpu.VMEM((owned // 2, lat_total, 2 * width), jnp.bfloat16),
            pltpu.VMEM((lat_total, owned, width), jnp.bfloat16),
            pltpu.SemaphoreType.DMA((6 + lat_total // 64 * 2,)),
        ],
        behind=2,
        away=True,
        room=100000,
    )
    filtered, *pieces = lax.optimization_barrier((filtered, north, upper, lower, south))
    returned = lax.all_to_all(
        filtered.reshape(owners, lats, owned, width), OWNERS, 0, 0, tiled=True
    )
    first_col = lax.axis_index(LON) * sea_cols
    kernels = jnp.broadcast_to(
        ocean_kernel.astype(jnp.float32).reshape(2, STENCIL_TAPS**2, 1, sea_width),
        (2, STENCIL_TAPS**2, 8, sea_width),
    )
    ocean = (kernels, ocean_gain, ocean_up, ocean_down)
    upper, lower = ocean_block(first_col - LEAD, circle, pieces, *ocean, 0, 2)
    north, south = shifted(lower, 1, 0), shifted(upper, -1, 0)
    returned, *pieces = lax.optimization_barrier((returned, north, upper, lower, south))
    spatial = waves(
        (lon_count, lats, lon_dev, width), inverse, returned, lax.ppermute(returned, "comp", swap)
    )
    spatial, *pieces = lax.optimization_barrier((spatial, *pieces))
    spectral = lax.all_to_all(spatial, LON, 0, 0, tiled=True).reshape(lat_dev, lon_dev, width)
    (current,) = ocean_block(first_col, circle, pieces, *ocean, 1, 1)
    ocean_out = jnp.where(wet_mask[:, :, None] == 1, current, ocean_state)
    spectral, ocean_out = lax.optimization_barrier((spectral, ocean_out))
    atm_out = epilogue(
        atm_state, flux_here, spectral, surface_to_atm, atm_gain[1:], atm_up, atm_down
    )
    return (atm_out, ocean_out)


def solution(mesh):
    lat_count, lon_count = mesh.shape["lat"], mesh.shape["lon"]
    torus = Mesh(
        mesh.devices.reshape(4, lat_count // 4, lon_count // 4, 4, mesh.shape["comp"]), ALL
    )
    atm, sea = P(LAT, (*LON, "comp"), None), P((*LAT, "comp"), LON, None)
    placed = (atm, sea, P((*LAT, "comp"), LON), P(ALL, None, None)) + (P(),) * 15
    return jax.shard_map(
        local, mesh=torus, in_specs=placed, out_specs=(atm, sea), check_vma=False
    )
```

```python
import functools
import math

import jax
import jax.numpy as jnp
import ml_dtypes
import numpy as np
from jax import lax
from jax.experimental import pallas as pl
from jax.experimental.pallas import tpu as pltpu
from jax.sharding import Mesh
from jax.sharding import PartitionSpec as P

MODES = 512
STENCIL_TAPS = 7
OCEAN_DILATION = 2
LAT = ("y", "z_hi")
LON = ("z_lo", "x")
ALL = (*LAT, *LON, "comp")
OWNERS = ("z_hi", "z_lo", "x", "y")


epsilon = 1e-05


def owner_order():
    count = lax.axis_size(LAT) * lax.axis_size(LON)
    return np.arange(count).reshape(lax.axis_size("y"), -1).T.reshape(-1)


def wave_tables(owners, lon_count, circle, owned):
    rows = (owners[:, None] * owned + np.arange(owned)).reshape(-1)
    block = circle // (2 * lon_count)
    where = np.arange(lon_count * block)
    forward, inverse = [], []
    row_sets = [rows // owned * 2 * owned + q * owned + rows % owned for q in range(2)]
    place_sets = [(where // block * 2 + q) * block + where % block for q in range(2)]

    def waves(row, place):
        phase = (row[:, None] // 2) * place[None, :] % circle
        angle = phase.astype(np.float32) * np.float32(2.0 * math.pi / circle)
        return np.where((row % 2 == 0)[:, None], np.cos(angle), -np.sin(angle)).astype(np.float32)

    for own in range(2):
        order = (own, 1 - own)
        f = np.concatenate([waves(row_sets[own], place_sets[q]) for q in order], 1)
        forward.append(f / np.float32(math.sqrt(circle)))
        g = []
        for q in order:
            factor = np.where(row_sets[q] // 2 == 0, 1.0, 2.0).astype(np.float32)
            g.append((waves(row_sets[q], place_sets[own]) * factor[:, None]).T)
        inverse.append(np.concatenate(g, 1) / np.float32(math.sqrt(circle)))
    return (
        np.stack(forward).astype(ml_dtypes.bfloat16),
        np.stack(inverse).astype(ml_dtypes.bfloat16),
    )


def waves_kernel(
    table_hbm, own_hbm, other_hbm, out_hbm, table_ref, own_ref, other_ref, held, sems
):
    lats, width = own_ref.shape[0], own_ref.shape[3]
    half = table_ref.shape[1] // 2
    table = pltpu.make_async_copy(table_hbm, table_ref, sems.at[0])
    table.start()
    owns, others, sends = [], [], []
    for i in range(lats):
        owns.append(pltpu.make_async_copy(own_hbm.at[:, i], own_ref.at[i], sems.at[1 + i]))
        owns[-1].start()
        at = sems.at[1 + lats + i]
        others.append(pltpu.make_async_copy(other_hbm.at[:, i], other_ref.at[i], at))
        others[-1].start()
    table.wait()
    for i in range(lats):
        owns[i].wait()
        total = jnp.dot(
            table_ref[:, :half],
            own_ref[i].reshape(half, width),
            preferred_element_type=jnp.float32,
        )
        others[i].wait()
        total += jnp.dot(
            table_ref[:, half:],
            other_ref[i].reshape(half, width),
            preferred_element_type=jnp.float32,
        )
        held[i] = total.astype(jnp.bfloat16).reshape(held.shape[1:])
        at = sems.at[1 + 2 * lats + i]
        sends.append(pltpu.make_async_copy(held.at[i], out_hbm.at[:, i], at))
        sends[-1].start()
    for send in sends:
        send.wait()


def waves(shape, table, own, other):
    lats = shape[1]
    return call(
        waves_kernel,
        shape,
        table,
        own,
        other,
        scratch=[
            pltpu.VMEM(table.shape, jnp.bfloat16),
            pltpu.VMEM((lats, own.shape[0], *own.shape[2:]), jnp.bfloat16),
            pltpu.VMEM((lats, own.shape[0], *own.shape[2:]), jnp.bfloat16),
            pltpu.VMEM((lats, shape[0], *shape[2:]), jnp.bfloat16),
            pltpu.SemaphoreType.DMA((1 + 3 * lats,)),
        ],
        behind=3,
        away=True,
    )


def prepare_kernel(
    legendre_ref, moved_ref, weight_ref, real_ref, imag_ref, weighted_ref, turned_ref, mix_ref
):
    width = real_ref.shape[0]
    for m in range(legendre_ref.shape[0]):
        table = jnp.dot(legendre_ref[m], moved_ref[...], preferred_element_type=jnp.float32)
        weighted_ref[m] = (table * weight_ref[...]).astype(jnp.bfloat16)
        turned_ref[m] = jnp.transpose(table).astype(jnp.bfloat16)
    mix_ref[:width, :width] = real_ref[...]
    mix_ref[:width, width:] = imag_ref[...]
    mix_ref[width:, :width] = -imag_ref[...]
    mix_ref[width:, width:] = real_ref[...]


def prepare(legendre, moved, weight, real, imag):
    count, degrees, lats = legendre.shape
    shapes = ((count, degrees, lats), (count, lats, degrees), (2 * real.shape[0],) * 2)
    here = pl.BlockSpec(memory_space=pltpu.VMEM)
    return pl.pallas_call(
        prepare_kernel,
        out_shape=[jax.ShapeDtypeStruct(shape, jnp.bfloat16) for shape in shapes],
        in_specs=[here] * 5,
        out_specs=[here] * 3,
        compiler_params=pltpu.CompilerParams(vmem_limit_bytes=VMEM - 38_000_000),
    )(legendre, moved, weight, real, imag)


def filter_kernel(
    gain_ref,
    spectrum_hbm,
    weighted_hbm,
    mix_hbm,
    turned_hbm,
    out_hbm,
    spectrum_ref,
    weighted_ref,
    mix_ref,
    turned_ref,
    rows_ref,
    held,
    sems,
):
    count = weighted_ref.shape[0]
    lats, owned, width = spectrum_ref.shape
    block = 64
    side = block * owned
    parts = lats // block
    pairs = ((weighted_hbm, weighted_ref), (mix_hbm, mix_ref), (turned_hbm, turned_ref))
    arrivals = []
    for b in range(parts):
        part = pl.ds(b * block, block)
        at = sems.at[len(pairs) + b]
        arrivals.append(pltpu.make_async_copy(spectrum_hbm.at[part], spectrum_ref.at[part], at))
        arrivals[-1].start()
    fetches = [
        pltpu.make_async_copy(source, target, sems.at[n])
        for n, (source, target) in enumerate(pairs)
    ]
    for fetch in fetches:
        fetch.start()
    r = lax.broadcasted_iota(jnp.int32, (side, side), 0)
    s = lax.broadcasted_iota(jnp.int32, (side, side), 1)
    pick = jnp.where((r % block) * owned + r // block == s, 1.0, 0.0).astype(jnp.bfloat16)
    back = jnp.where((s % block) * owned + s // block == r, 1.0, 0.0).astype(jnp.bfloat16)

    def columns(p):
        return slice(p % 2 * width, (p % 2 + 1) * width)

    for b in range(parts):
        span = slice(b * block, (b + 1) * block)
        arrivals[b].wait()
        piece = spectrum_ref[span].reshape(side, width)
        moved = jnp.dot(pick, piece, preferred_element_type=jnp.float32).astype(jnp.bfloat16)
        for p in range(owned):
            rows_ref[p // 2, span, columns(p)] = moved[p * block : (p + 1) * block]
    gain = jnp.transpose(jnp.broadcast_to(gain_ref[...], (8, lats)))[:, :1]
    for fetch in fetches:
        fetch.wait()
    for m in range(count):
        coeffs = jnp.dot(weighted_ref[m], rows_ref[m], preferred_element_type=jnp.float32)
        mixed = jnp.dot(
            coeffs.astype(jnp.bfloat16), mix_ref[...], preferred_element_type=jnp.float32
        )
        filtered = (mixed * gain).astype(jnp.bfloat16)
        rows_ref[m] = jnp.dot(
            turned_ref[m], filtered, preferred_element_type=jnp.float32
        ).astype(jnp.bfloat16)
    sends = []
    for b in range(parts):
        span = slice(b * block, (b + 1) * block)
        piece = jnp.concatenate(
            [rows_ref[p // 2, span, columns(p)] for p in range(owned)], axis=0
        )
        moved = jnp.dot(back, piece, preferred_element_type=jnp.float32).astype(jnp.bfloat16)
        held[span] = moved.reshape(block, owned, width)
        at = sems.at[len(pairs) + parts + b]
        part = pl.ds(b * block, block)
        sends.append(pltpu.make_async_copy(held.at[part], out_hbm.at[part], at))
        sends[-1].start()
    for send in sends:
        send.wait()


VMEM = 62_900_000


def call(kernel, shape, *args, scratch=(), room=0, scalars=0, behind=0, away=False):
    spaces = [pltpu.SMEM] * scalars + [pltpu.VMEM] * (len(args) - scalars - behind)
    spaces += [pltpu.HBM] * behind
    return pl.pallas_call(
        kernel,
        out_shape=jax.ShapeDtypeStruct(shape, jnp.bfloat16),
        in_specs=[pl.BlockSpec(memory_space=space) for space in spaces],
        out_specs=pl.BlockSpec(memory_space=pltpu.HBM if away else pltpu.VMEM),
        scratch_shapes=list(scratch),
        compiler_params=pltpu.CompilerParams(vmem_limit_bytes=VMEM - room),
    )(*args)


def gelu(x):
    inner = x * (math.sqrt(2.0 / math.pi) + (math.sqrt(2.0 / math.pi) * 0.044715) * (x * x))
    half = 0.5 * x
    return half + half * jnp.tanh(inner)


def normalised(values, gain):
    centred = values - jnp.mean(values, axis=-1, keepdims=True)
    spread = jnp.mean(centred * centred, axis=-1, keepdims=True)
    return (centred * lax.rsqrt(spread + epsilon) * gain).astype(jnp.bfloat16)


def prologue_kernel(atm_ref, flux_ref, out_weight_ref, gain_ref, out_hbm, held, sems):
    rows, lon_dev, width = atm_ref.shape
    each = rows // sems.shape[0]
    sends = []
    for k in range(sems.shape[0]):
        part = pl.ds(k * each, each)
        flux = flux_ref[pl.ds(k * each * lon_dev, each * lon_dev)]
        forced = atm_ref[part].reshape(each * lon_dev, width).astype(jnp.float32) + jnp.dot(
            flux, out_weight_ref[...], preferred_element_type=jnp.float32
        )
        held[part] = normalised(forced, gain_ref[...]).reshape(each, lon_dev, width)
        sends.append(pltpu.make_async_copy(held.at[part], out_hbm.at[part], sems.at[k]))
        sends[-1].start()
    for send in sends:
        send.wait()


def epilogue_kernel(
    atm_ref, flux_ref, spectral_ref, out_weight_ref, gain_ref, up_ref, down_ref, out_ref
):
    rows, lon_dev, width = atm_ref.shape
    each = rows // 2
    side = each * lon_dev
    for k in range(2):
        part = pl.ds(k * each, each)
        forced = atm_ref[part].reshape(side, width).astype(jnp.float32) + jnp.dot(
            flux_ref[pl.ds(k * side, side)],
            out_weight_ref[...],
            preferred_element_type=jnp.float32,
        )
        mixed = forced + spectral_ref[part].reshape(side, width).astype(jnp.float32)
        normed = normalised(mixed, gain_ref[...])
        hidden = gelu(jnp.dot(normed, up_ref[...], preferred_element_type=jnp.float32))
        total = mixed + jnp.dot(
            hidden.astype(jnp.bfloat16), down_ref[...], preferred_element_type=jnp.float32
        )
        out_ref[part] = total.astype(jnp.bfloat16).reshape(each, lon_dev, width)


def epilogue(atm, flux, spectral, *weights, rows=8):
    lat_dev, lon_dev, width = atm.shape
    field = pl.BlockSpec((rows, lon_dev, width), lambda i: (i, 0, 0))
    specs = [field, pl.BlockSpec((rows * lon_dev, flux.shape[1]), lambda i: (i, 0)), field]
    specs += [pl.BlockSpec(w.shape, lambda i: (0, 0)) for w in weights]
    return pl.pallas_call(
        epilogue_kernel,
        grid=(lat_dev // rows,),
        out_shape=jax.ShapeDtypeStruct(atm.shape, jnp.bfloat16),
        in_specs=specs,
        out_specs=field,
        compiler_params=pltpu.CompilerParams(vmem_limit_bytes=VMEM - 38000000),
    )(atm, flux, spectral, *weights)


HALO = 16
LEAD = 8
LANES = 128
REACH = STENCIL_TAPS // 2 * OCEAN_DILATION


def ocean_rows(field, kern, gain, up, down, sums, out_ref, group, low, high):
    blocks = field.shape[0]
    rows, cols, width = out_ref.shape
    stride = cols // 8
    each = stride // OCEAN_DILATION

    def step(g, carry):
        top = g * group
        for r in range(group):
            for lane in range(blocks):
                part = slice(lane * LANES, (lane + 1) * LANES)
                for parity in range(OCEAN_DILATION):
                    acc = [None] * each
                    for a in range(STENCIL_TAPS):
                        row = top + r + a * OCEAN_DILATION
                        first = LEAD - REACH + parity
                        loads = [
                            field[lane, row, pl.ds(first + OCEAN_DILATION * q, 8, stride=stride), :]
                            for q in range(each + STENCIL_TAPS - 1)
                        ]
                        for b in range(STENCIL_TAPS):
                            weight = kern[a * STENCIL_TAPS + b, :, part]
                            for q in range(each):
                                term = loads[q + b] * weight
                                acc[q] = term if acc[q] is None else acc[q] + term
                    for q in range(each):
                        at = pl.ds(parity + OCEAN_DILATION * q, 8, stride=stride)
                        sums[lane, r, at, :] = acc[q]
        side = group * cols
        stencil = jnp.concatenate(
            [sums[lane].reshape(side, LANES) for lane in range(blocks)], axis=1
        )
        normed = normalised(stencil, gain[...])
        hidden = gelu(jnp.dot(normed, up[...], preferred_element_type=jnp.float32))
        total = jnp.dot(
            hidden.astype(jnp.bfloat16), down[...], preferred_element_type=jnp.float32
        )
        for r in range(group):
            centre = jnp.concatenate(
                [field[lane, top + r + REACH, LEAD : LEAD + cols, :] for lane in range(blocks)],
                axis=1,
            )
            value = centre + total[r * cols : (r + 1) * cols]
            col = lax.broadcasted_iota(jnp.int32, value.shape, 0)
            value = jnp.where((col >= low) & (col < high), value, 0.0)
            out_ref[top + r] = value.astype(jnp.bfloat16)
        return carry

    lax.fori_loop(0, rows // group, step, 0)


def ocean_kernel(
    inside_ref,
    north_ref,
    upper_ref,
    lower_ref,
    south_ref,
    kern_ref,
    gain_ref,
    up_ref,
    down_ref,
    *rest,
    block,
):
    *outs, field, sums, held = rest
    at = 0
    for ref in (north_ref, upper_ref, lower_ref, south_ref):
        for lane in range(field.shape[0]):
            field[lane, at : at + ref.shape[0]] = ref[
                :, :, lane * LANES : (lane + 1) * LANES
            ].astype(jnp.float32)
        at += ref.shape[0]
    group = sums.shape[1]
    low, high = inside_ref[0], inside_ref[1]
    weights = (kern_ref.at[block], gain_ref, up_ref.at[block], down_ref.at[block])
    ocean_rows(field, *weights, sums, held, group, low, high)
    each = held.shape[0] // len(outs)
    for n, out in enumerate(outs):
        out[...] = held[n * each : (n + 1) * each]


def ocean_block(first_col, circle, pieces, kern, gain, up, down, block, parts):
    half, cols, width = pieces[0].shape
    blocks, out_cols, rows = width // LANES, cols - 2 * LEAD, 2 * half
    out = jax.ShapeDtypeStruct((rows // parts, out_cols, width), jnp.bfloat16)
    here = pl.BlockSpec(memory_space=pltpu.VMEM)
    return pl.pallas_call(
        functools.partial(ocean_kernel, block=block),
        out_shape=[out] * parts,
        in_specs=[pl.BlockSpec(memory_space=pltpu.SMEM), *[here] * 8],
        out_specs=[here] * parts,
        scratch_shapes=[
            pltpu.VMEM((blocks, rows + 2 * REACH, cols, LANES), jnp.float32),
            pltpu.VMEM((blocks, 4, out_cols, LANES), jnp.float32),
            pltpu.VMEM((rows, out_cols, width), jnp.bfloat16),
        ],
        compiler_params=pltpu.CompilerParams(vmem_limit_bytes=VMEM - 38_000_000),
    )(
        jnp.stack([-first_col, circle - first_col]).astype(jnp.int32),
        *pieces,
        kern,
        gain[block : block + 1],
        up,
        down,
    )


def shifted(block, dy, dx):
    tall = lax.axis_size(LAT) * lax.axis_size("comp")
    broad = lax.axis_size(LON)

    def place(y, x):
        return (y // 2 * broad + x) * 2 + y % 2

    pairs = [
        (place(y, x), place(y + dy, x + dx))
        for y in range(tall)
        for x in range(broad)
        if 0 <= y + dy < tall and 0 <= x + dx < broad
    ]
    return lax.ppermute(block, ALL, pairs)


def local(
    atm_state,
    ocean_state,
    wet_mask,
    legendre,
    quad_weight,
    spec_real,
    spec_imag,
    degree_gain,
    atm_gain,
    atm_up,
    atm_down,
    atm_to_surface,
    surface_to_atm,
    ocean_to_surface,
    surface_to_ocean,
    ocean_kernel,
    ocean_gain,
    ocean_up,
    ocean_down,
):
    lat_count = lax.axis_size(LAT)
    lon_count = lax.axis_size(LON)
    lat_dev, lon_dev, width = atm_state.shape
    sea_rows, sea_cols, sea_width = ocean_state.shape
    lat_total = lat_dev * lat_count
    circle = lon_dev * lon_count * 2
    owned = 2 * legendre.shape[0]
    owners = lat_count * lon_count
    order = owner_order()
    lats = lat_dev // lon_count
    me = lax.axis_index("comp")
    swap = [(0, 1), (1, 0)]
    forward, inverse = wave_tables(order, lon_count, circle, owned)
    forward = lax.dynamic_index_in_dim(jnp.asarray(forward), me, 0, keepdims=False)
    inverse = lax.dynamic_index_in_dim(jnp.asarray(inverse), me, 0, keepdims=False)
    wet = wet_mask.astype(jnp.float32)[:, :, None]
    ocean_flux = (
        jnp.dot(ocean_state, ocean_to_surface, preferred_element_type=jnp.float32) * wet
    ).astype(jnp.bfloat16)
    atm_flux = jnp.dot(atm_state, atm_to_surface, preferred_element_type=jnp.float32).astype(
        jnp.bfloat16
    )

    def halves(mine, dim):
        low, high = jnp.split(mine, 2, axis=dim)
        return (jnp.where(me == 0, low, high), jnp.where(me == 0, high, low))

    def together(kept, got, dim):
        low = jnp.where(me == 0, kept, got)
        high = jnp.where(me == 0, got, kept)
        return jnp.concatenate([low, high], axis=dim)

    kept_ocean, sent_ocean = halves(ocean_flux, 1)
    kept_atm, sent_atm = halves(atm_flux, 0)
    got_ocean = lax.ppermute(sent_ocean, "comp", swap)
    flux_here = together(kept_ocean, got_ocean, 0).reshape(lat_dev * lon_dev, -1)
    normed = call(
        prologue_kernel,
        atm_state.shape,
        atm_state,
        flux_here,
        surface_to_atm,
        atm_gain[:1],
        scratch=[pltpu.VMEM(atm_state.shape, jnp.bfloat16), pltpu.SemaphoreType.DMA((3,))],
        away=True,
        room=24000000,
    )
    rings = lax.all_to_all(
        normed.reshape(lon_count, lats, lon_dev, width), LON, 0, 0, tiled=True
    )
    flux_sea = together(kept_atm, lax.ppermute(sent_atm, "comp", swap), 1)
    ocean_in = (
        ocean_state.astype(jnp.float32)
        + wet * jnp.dot(flux_sea, surface_to_ocean, preferred_element_type=jnp.float32)
    ).astype(jnp.bfloat16)
    west = shifted(ocean_in[:, -HALO:], 0, 1)
    east = shifted(ocean_in[:, :HALO], 0, -1)
    upper, lower = [
        jnp.concatenate([west[part], ocean_in[part], east[part]], axis=1)
        for part in (slice(0, REACH), slice(REACH, None))
    ]
    seen = (order[:, None] * lats + np.arange(lats)).reshape(-1)
    moved = jnp.asarray(np.eye(lat_total)[:, seen].astype(ml_dtypes.bfloat16))
    weight = quad_weight.reshape(lax.axis_size("y"), -1, lats).swapaxes(0, 1).reshape(1, -1)
    weighted, turned, mix = prepare(legendre, moved, weight / lat_total, spec_real, spec_imag)
    gain_row = degree_gain[None]
    rings, upper, lower, weighted, turned, mix, gain_row = lax.optimization_barrier(
        (rings, upper, lower, weighted, turned, mix, gain_row)
    )
    north, south = shifted(lower, 1, 0), shifted(upper, -1, 0)
    spectrum = waves(
        (owners, lats, owned, width), forward, rings, lax.ppermute(rings, "comp", swap)
    )
    spectrum, *pieces = lax.optimization_barrier((spectrum, north, upper, lower, south))
    gathered = lax.all_to_all(spectrum, OWNERS, 0, 0, tiled=True)
    first_col = lax.axis_index(LON) * sea_cols
    kernels = jnp.broadcast_to(
        ocean_kernel.astype(jnp.float32).reshape(2, STENCIL_TAPS**2, 1, sea_width),
        (2, STENCIL_TAPS**2, 8, sea_width),
    )
    ocean = (kernels, ocean_gain, ocean_up, ocean_down)
    upper, lower = ocean_block(first_col - LEAD, circle, pieces, *ocean, 0, 2)
    gathered, upper, lower = lax.optimization_barrier((gathered, upper, lower))
    north, south = shifted(lower, 1, 0), shifted(upper, -1, 0)
    filtered = call(
        filter_kernel,
        (lat_total, owned, width),
        gain_row,
        gathered.reshape(lat_total, owned, width),
        weighted,
        mix,
        turned,
        scratch=[
            pltpu.VMEM((lat_total, owned, width), jnp.bfloat16),
            pltpu.VMEM(weighted.shape, jnp.bfloat16),
            pltpu.VMEM((2 * width, 2 * width), jnp.bfloat16),
            pltpu.VMEM(turned.shape, jnp.bfloat16),
            pltpu.VMEM((owned // 2, lat_total, 2 * width), jnp.bfloat16),
            pltpu.VMEM((lat_total, owned, width), jnp.bfloat16),
            pltpu.SemaphoreType.DMA((3 + lat_total // 64 * 2,)),
        ],
        behind=4,
        away=True,
        room=100_000,
    )
    filtered, *pieces = lax.optimization_barrier((filtered, north, upper, lower, south))
    returned = lax.all_to_all(
        filtered.reshape(owners, lats, owned, width), OWNERS, 0, 0, tiled=True
    )
    (current,) = ocean_block(first_col, circle, pieces, *ocean, 1, 1)
    ocean_out = jnp.where(wet_mask[:, :, None] == 1, current, ocean_state)
    returned, ocean_out = lax.optimization_barrier((returned, ocean_out))
    spatial = waves(
        (lon_count, lats, lon_dev, width), inverse, returned, lax.ppermute(returned, "comp", swap)
    )
    spectral = lax.all_to_all(spatial, LON, 0, 0, tiled=True).reshape(lat_dev, lon_dev, width)
    atm_out = epilogue(
        atm_state, flux_here, spectral, surface_to_atm, atm_gain[1:], atm_up, atm_down
    )
    return (atm_out, ocean_out)


def solution(mesh):
    lat_count, lon_count = mesh.shape["lat"], mesh.shape["lon"]
    torus = Mesh(
        mesh.devices.reshape(4, lat_count // 4, lon_count // 4, 4, mesh.shape["comp"]), ALL
    )
    atm, sea = P(LAT, (*LON, "comp"), None), P((*LAT, "comp"), LON, None)
    placed = (atm, sea, P((*LAT, "comp"), LON), P(ALL, None, None)) + (P(),) * 15
    return jax.shard_map(
        local, mesh=torus, in_specs=placed, out_specs=(atm, sea), check_vma=False
    )
```

```python
import functools
import math

import jax
import jax.numpy as jnp
import ml_dtypes
import numpy as np
from jax import lax
from jax.experimental import pallas as pl
from jax.experimental.pallas import tpu as pltpu
from jax.sharding import Mesh
from jax.sharding import PartitionSpec as P

MODES = 512
STENCIL_TAPS = 7
OCEAN_DILATION = 2
LAT = ("y", "z_hi")
LON = ("z_lo", "x")
ALL = (*LAT, *LON, "comp")
OWNERS = ("z_hi", "z_lo", "x", "y")


epsilon = 1e-05


def owner_order():
    count = lax.axis_size(LAT) * lax.axis_size(LON)
    return np.arange(count).reshape(lax.axis_size("y"), -1).T.reshape(-1)


def wave_tables(owners, lon_count, circle, owned):
    rows = (owners[:, None] * owned + np.arange(owned)).reshape(-1)
    block = circle // (2 * lon_count)
    where = np.arange(lon_count * block)
    forward, inverse = [], []
    row_sets = [rows // owned * 2 * owned + q * owned + rows % owned for q in range(2)]
    place_sets = [(where // block * 2 + q) * block + where % block for q in range(2)]

    def waves(row, place):
        phase = (row[:, None] // 2) * place[None, :] % circle
        angle = phase.astype(np.float32) * np.float32(2.0 * math.pi / circle)
        return np.where((row % 2 == 0)[:, None], np.cos(angle), -np.sin(angle)).astype(np.float32)

    for own in range(2):
        order = (own, 1 - own)
        f = np.concatenate([waves(row_sets[own], place_sets[q]) for q in order], 1)
        forward.append(f / np.float32(math.sqrt(circle)))
        g = []
        for q in order:
            factor = np.where(row_sets[q] // 2 == 0, 1.0, 2.0).astype(np.float32)
            g.append((waves(row_sets[q], place_sets[own]) * factor[:, None]).T)
        inverse.append(np.concatenate(g, 1) / np.float32(math.sqrt(circle)))
    return (
        np.stack(forward).astype(ml_dtypes.bfloat16),
        np.stack(inverse).astype(ml_dtypes.bfloat16),
    )


def waves_kernel(
    table_hbm, own_hbm, other_hbm, out_hbm, table_ref, own_ref, other_ref, held, sems
):
    lats, width = own_ref.shape[0], own_ref.shape[3]
    half = table_ref.shape[1] // 2
    table = pltpu.make_async_copy(table_hbm, table_ref, sems.at[0])
    table.start()
    owns, others, sends = [], [], []
    for i in range(lats):
        owns.append(pltpu.make_async_copy(own_hbm.at[:, i], own_ref.at[i], sems.at[1 + i]))
        owns[-1].start()
        at = sems.at[1 + lats + i]
        others.append(pltpu.make_async_copy(other_hbm.at[:, i], other_ref.at[i], at))
        others[-1].start()
    table.wait()
    for i in range(lats):
        owns[i].wait()
        total = jnp.dot(
            table_ref[:, :half],
            own_ref[i].reshape(half, width),
            preferred_element_type=jnp.float32,
        )
        others[i].wait()
        total += jnp.dot(
            table_ref[:, half:],
            other_ref[i].reshape(half, width),
            preferred_element_type=jnp.float32,
        )
        held[i] = total.astype(jnp.bfloat16).reshape(held.shape[1:])
        at = sems.at[1 + 2 * lats + i]
        sends.append(pltpu.make_async_copy(held.at[i], out_hbm.at[:, i], at))
        sends[-1].start()
    for send in sends:
        send.wait()


def waves(shape, table, own, other):
    lats = shape[1]
    return call(
        waves_kernel,
        shape,
        table,
        own,
        other,
        scratch=[
            pltpu.VMEM(table.shape, jnp.bfloat16),
            pltpu.VMEM((lats, own.shape[0], *own.shape[2:]), jnp.bfloat16),
            pltpu.VMEM((lats, own.shape[0], *own.shape[2:]), jnp.bfloat16),
            pltpu.VMEM((lats, shape[0], *shape[2:]), jnp.bfloat16),
            pltpu.SemaphoreType.DMA((1 + 3 * lats,)),
        ],
        behind=3,
        away=True,
    )


def prepare_kernel(
    legendre_ref, moved_ref, weight_ref, real_ref, imag_ref, weighted_ref, turned_ref, mix_ref
):
    width = real_ref.shape[0]
    for m in range(legendre_ref.shape[0]):
        table = jnp.dot(legendre_ref[m], moved_ref[...], preferred_element_type=jnp.float32)
        weighted_ref[m] = (table * weight_ref[...]).astype(jnp.bfloat16)
        turned_ref[m] = jnp.transpose(table).astype(jnp.bfloat16)
    mix_ref[:width, :width] = real_ref[...]
    mix_ref[:width, width:] = imag_ref[...]
    mix_ref[width:, :width] = -imag_ref[...]
    mix_ref[width:, width:] = real_ref[...]


def prepare(legendre, moved, weight, real, imag):
    count, degrees, lats = legendre.shape
    shapes = ((count, degrees, lats), (count, lats, degrees), (2 * real.shape[0],) * 2)
    here = pl.BlockSpec(memory_space=pltpu.VMEM)
    return pl.pallas_call(
        prepare_kernel,
        out_shape=[jax.ShapeDtypeStruct(shape, jnp.bfloat16) for shape in shapes],
        in_specs=[here] * 5,
        out_specs=[here] * 3,
        compiler_params=pltpu.CompilerParams(vmem_limit_bytes=VMEM - 38_000_000),
    )(legendre, moved, weight, real, imag)


def filter_kernel(
    gain_ref,
    spectrum_hbm,
    weighted_hbm,
    mix_hbm,
    turned_hbm,
    out_hbm,
    spectrum_ref,
    weighted_ref,
    mix_ref,
    turned_ref,
    rows_ref,
    held,
    sems,
):
    count = weighted_ref.shape[0]
    lats, owned, width = spectrum_ref.shape
    block = 64
    side = block * owned
    parts = lats // block
    pairs = ((weighted_hbm, weighted_ref), (mix_hbm, mix_ref), (turned_hbm, turned_ref))
    arrivals = []
    for b in range(parts):
        part = pl.ds(b * block, block)
        at = sems.at[len(pairs) + b]
        arrivals.append(pltpu.make_async_copy(spectrum_hbm.at[part], spectrum_ref.at[part], at))
        arrivals[-1].start()
    fetches = [
        pltpu.make_async_copy(source, target, sems.at[n])
        for n, (source, target) in enumerate(pairs)
    ]
    for fetch in fetches:
        fetch.start()
    r = lax.broadcasted_iota(jnp.int32, (side, side), 0)
    s = lax.broadcasted_iota(jnp.int32, (side, side), 1)
    pick = jnp.where((r % block) * owned + r // block == s, 1.0, 0.0).astype(jnp.bfloat16)
    back = jnp.where((s % block) * owned + s // block == r, 1.0, 0.0).astype(jnp.bfloat16)

    def columns(p):
        return slice(p % 2 * width, (p % 2 + 1) * width)

    for b in range(parts):
        span = slice(b * block, (b + 1) * block)
        arrivals[b].wait()
        piece = spectrum_ref[span].reshape(side, width)
        moved = jnp.dot(pick, piece, preferred_element_type=jnp.float32).astype(jnp.bfloat16)
        for p in range(owned):
            rows_ref[p // 2, span, columns(p)] = moved[p * block : (p + 1) * block]
    gain = jnp.transpose(jnp.broadcast_to(gain_ref[...], (8, lats)))[:, :1]
    for fetch in fetches:
        fetch.wait()
    for m in range(count):
        coeffs = jnp.dot(weighted_ref[m], rows_ref[m], preferred_element_type=jnp.float32)
        mixed = jnp.dot(
            coeffs.astype(jnp.bfloat16), mix_ref[...], preferred_element_type=jnp.float32
        )
        filtered = (mixed * gain).astype(jnp.bfloat16)
        rows_ref[m] = jnp.dot(
            turned_ref[m], filtered, preferred_element_type=jnp.float32
        ).astype(jnp.bfloat16)
    sends = []
    for b in range(parts):
        span = slice(b * block, (b + 1) * block)
        piece = jnp.concatenate(
            [rows_ref[p // 2, span, columns(p)] for p in range(owned)], axis=0
        )
        moved = jnp.dot(back, piece, preferred_element_type=jnp.float32).astype(jnp.bfloat16)
        held[span] = moved.reshape(block, owned, width)
        at = sems.at[len(pairs) + parts + b]
        part = pl.ds(b * block, block)
        sends.append(pltpu.make_async_copy(held.at[part], out_hbm.at[part], at))
        sends[-1].start()
    for send in sends:
        send.wait()


VMEM = 62_900_000


def call(kernel, shape, *args, scratch=(), room=0, scalars=0, behind=0, away=False):
    spaces = [pltpu.SMEM] * scalars + [pltpu.VMEM] * (len(args) - scalars - behind)
    spaces += [pltpu.HBM] * behind
    return pl.pallas_call(
        kernel,
        out_shape=jax.ShapeDtypeStruct(shape, jnp.bfloat16),
        in_specs=[pl.BlockSpec(memory_space=space) for space in spaces],
        out_specs=pl.BlockSpec(memory_space=pltpu.HBM if away else pltpu.VMEM),
        scratch_shapes=list(scratch),
        compiler_params=pltpu.CompilerParams(vmem_limit_bytes=VMEM - room),
    )(*args)


def gelu(x):
    inner = x * (math.sqrt(2.0 / math.pi) + (math.sqrt(2.0 / math.pi) * 0.044715) * (x * x))
    half = 0.5 * x
    return half + half * jnp.tanh(inner)


def normalised(values, gain):
    centred = values - jnp.mean(values, axis=-1, keepdims=True)
    spread = jnp.mean(centred * centred, axis=-1, keepdims=True)
    return (centred * lax.rsqrt(spread + epsilon) * gain).astype(jnp.bfloat16)


def prologue_kernel(atm_ref, flux_ref, out_weight_ref, gain_ref, out_hbm, held, sems):
    rows, lon_dev, width = atm_ref.shape
    each = rows // sems.shape[0]
    sends = []
    for k in range(sems.shape[0]):
        part = pl.ds(k * each, each)
        flux = flux_ref[pl.ds(k * each * lon_dev, each * lon_dev)]
        forced = atm_ref[part].reshape(each * lon_dev, width).astype(jnp.float32) + jnp.dot(
            flux, out_weight_ref[...], preferred_element_type=jnp.float32
        )
        held[part] = normalised(forced, gain_ref[...]).reshape(each, lon_dev, width)
        sends.append(pltpu.make_async_copy(held.at[part], out_hbm.at[part], sems.at[k]))
        sends[-1].start()
    for send in sends:
        send.wait()


def epilogue_kernel(
    atm_ref, flux_ref, spectral_ref, out_weight_ref, gain_ref, up_ref, down_ref, out_ref
):
    rows, lon_dev, width = atm_ref.shape
    each = rows // 2
    side = each * lon_dev
    for k in range(2):
        part = pl.ds(k * each, each)
        forced = atm_ref[part].reshape(side, width).astype(jnp.float32) + jnp.dot(
            flux_ref[pl.ds(k * side, side)],
            out_weight_ref[...],
            preferred_element_type=jnp.float32,
        )
        mixed = forced + spectral_ref[part].reshape(side, width).astype(jnp.float32)
        normed = normalised(mixed, gain_ref[...])
        hidden = gelu(jnp.dot(normed, up_ref[...], preferred_element_type=jnp.float32))
        total = mixed + jnp.dot(
            hidden.astype(jnp.bfloat16), down_ref[...], preferred_element_type=jnp.float32
        )
        out_ref[part] = total.astype(jnp.bfloat16).reshape(each, lon_dev, width)


def epilogue(atm, flux, spectral, *weights, rows=8):
    lat_dev, lon_dev, width = atm.shape
    field = pl.BlockSpec((rows, lon_dev, width), lambda i: (i, 0, 0))
    specs = [field, pl.BlockSpec((rows * lon_dev, flux.shape[1]), lambda i: (i, 0)), field]
    specs += [pl.BlockSpec(w.shape, lambda i: (0, 0)) for w in weights]
    return pl.pallas_call(
        epilogue_kernel,
        grid=(lat_dev // rows,),
        out_shape=jax.ShapeDtypeStruct(atm.shape, jnp.bfloat16),
        in_specs=specs,
        out_specs=field,
        compiler_params=pltpu.CompilerParams(vmem_limit_bytes=VMEM - 38000000),
    )(atm, flux, spectral, *weights)


HALO = 16
LEAD = 8
LANES = 128
REACH = STENCIL_TAPS // 2 * OCEAN_DILATION


def ocean_rows(field, kern, gain, up, down, sums, out_ref, group, low, high):
    blocks = field.shape[0]
    rows, cols, width = out_ref.shape
    stride = cols // 8
    each = stride // OCEAN_DILATION

    def step(g, carry):
        top = g * group
        for r in range(group):
            for lane in range(blocks):
                part = slice(lane * LANES, (lane + 1) * LANES)
                for parity in range(OCEAN_DILATION):
                    acc = [None] * each
                    for a in range(STENCIL_TAPS):
                        row = top + r + a * OCEAN_DILATION
                        first = LEAD - REACH + parity
                        loads = [
                            field[lane, row, pl.ds(first + OCEAN_DILATION * q, 8, stride=stride), :]
                            for q in range(each + STENCIL_TAPS - 1)
                        ]
                        for b in range(STENCIL_TAPS):
                            weight = kern[a * STENCIL_TAPS + b, :, part]
                            for q in range(each):
                                term = loads[q + b] * weight
                                acc[q] = term if acc[q] is None else acc[q] + term
                    for q in range(each):
                        at = pl.ds(parity + OCEAN_DILATION * q, 8, stride=stride)
                        sums[lane, r, at, :] = acc[q]
        side = group * cols
        stencil = jnp.concatenate(
            [sums[lane].reshape(side, LANES) for lane in range(blocks)], axis=1
        )
        normed = normalised(stencil, gain[...])
        hidden = gelu(jnp.dot(normed, up[...], preferred_element_type=jnp.float32))
        total = jnp.dot(
            hidden.astype(jnp.bfloat16), down[...], preferred_element_type=jnp.float32
        )
        for r in range(group):
            centre = jnp.concatenate(
                [field[lane, top + r + REACH, LEAD : LEAD + cols, :] for lane in range(blocks)],
                axis=1,
            )
            value = centre + total[r * cols : (r + 1) * cols]
            col = lax.broadcasted_iota(jnp.int32, value.shape, 0)
            value = jnp.where((col >= low) & (col < high), value, 0.0)
            out_ref[top + r] = value.astype(jnp.bfloat16)
        return carry

    lax.fori_loop(0, rows // group, step, 0)


def ocean_kernel(
    inside_ref,
    north_ref,
    upper_ref,
    lower_ref,
    south_ref,
    kern_ref,
    gain_ref,
    up_ref,
    down_ref,
    *rest,
    block,
):
    *outs, field, sums, held = rest
    at = 0
    for ref in (north_ref, upper_ref, lower_ref, south_ref):
        for lane in range(field.shape[0]):
            field[lane, at : at + ref.shape[0]] = ref[
                :, :, lane * LANES : (lane + 1) * LANES
            ].astype(jnp.float32)
        at += ref.shape[0]
    group = sums.shape[1]
    low, high = inside_ref[0], inside_ref[1]
    weights = (kern_ref.at[block], gain_ref, up_ref.at[block], down_ref.at[block])
    ocean_rows(field, *weights, sums, held, group, low, high)
    each = held.shape[0] // len(outs)
    for n, out in enumerate(outs):
        out[...] = held[n * each : (n + 1) * each]


def ocean_block(first_col, circle, pieces, kern, gain, up, down, block, parts):
    half, cols, width = pieces[0].shape
    blocks, out_cols, rows = width // LANES, cols - 2 * LEAD, 2 * half
    out = jax.ShapeDtypeStruct((rows // parts, out_cols, width), jnp.bfloat16)
    here = pl.BlockSpec(memory_space=pltpu.VMEM)
    return pl.pallas_call(
        functools.partial(ocean_kernel, block=block),
        out_shape=[out] * parts,
        in_specs=[pl.BlockSpec(memory_space=pltpu.SMEM), *[here] * 8],
        out_specs=[here] * parts,
        scratch_shapes=[
            pltpu.VMEM((blocks, rows + 2 * REACH, cols, LANES), jnp.float32),
            pltpu.VMEM((blocks, 4, out_cols, LANES), jnp.float32),
            pltpu.VMEM((rows, out_cols, width), jnp.bfloat16),
        ],
        compiler_params=pltpu.CompilerParams(vmem_limit_bytes=VMEM - 38_000_000),
    )(
        jnp.stack([-first_col, circle - first_col]).astype(jnp.int32),
        *pieces,
        kern,
        gain[block : block + 1],
        up,
        down,
    )


def shifted(block, dy, dx):
    tall = lax.axis_size(LAT) * lax.axis_size("comp")
    broad = lax.axis_size(LON)

    def place(y, x):
        return (y // 2 * broad + x) * 2 + y % 2

    pairs = [
        (place(y, x), place(y + dy, x + dx))
        for y in range(tall)
        for x in range(broad)
        if 0 <= y + dy < tall and 0 <= x + dx < broad
    ]
    return lax.ppermute(block, ALL, pairs)


def local(
    atm_state,
    ocean_state,
    wet_mask,
    legendre,
    quad_weight,
    spec_real,
    spec_imag,
    degree_gain,
    atm_gain,
    atm_up,
    atm_down,
    atm_to_surface,
    surface_to_atm,
    ocean_to_surface,
    surface_to_ocean,
    ocean_kernel,
    ocean_gain,
    ocean_up,
    ocean_down,
):
    lat_count = lax.axis_size(LAT)
    lon_count = lax.axis_size(LON)
    lat_dev, lon_dev, width = atm_state.shape
    sea_rows, sea_cols, sea_width = ocean_state.shape
    lat_total = lat_dev * lat_count
    circle = lon_dev * lon_count * 2
    owned = 2 * legendre.shape[0]
    owners = lat_count * lon_count
    order = owner_order()
    lats = lat_dev // lon_count
    me = lax.axis_index("comp")
    swap = [(0, 1), (1, 0)]
    forward, inverse = wave_tables(order, lon_count, circle, owned)
    forward = lax.dynamic_index_in_dim(jnp.asarray(forward), me, 0, keepdims=False)
    inverse = lax.dynamic_index_in_dim(jnp.asarray(inverse), me, 0, keepdims=False)
    wet = wet_mask.astype(jnp.float32)[:, :, None]
    ocean_flux = (
        jnp.dot(ocean_state, ocean_to_surface, preferred_element_type=jnp.float32) * wet
    ).astype(jnp.bfloat16)
    atm_flux = jnp.dot(atm_state, atm_to_surface, preferred_element_type=jnp.float32).astype(
        jnp.bfloat16
    )

    def halves(mine, dim):
        low, high = jnp.split(mine, 2, axis=dim)
        return (jnp.where(me == 0, low, high), jnp.where(me == 0, high, low))

    def together(kept, got, dim):
        low = jnp.where(me == 0, kept, got)
        high = jnp.where(me == 0, got, kept)
        return jnp.concatenate([low, high], axis=dim)

    kept_ocean, sent_ocean = halves(ocean_flux, 1)
    kept_atm, sent_atm = halves(atm_flux, 0)
    got_ocean = lax.ppermute(sent_ocean, "comp", swap)
    flux_here = together(kept_ocean, got_ocean, 0).reshape(lat_dev * lon_dev, -1)
    normed = call(
        prologue_kernel,
        atm_state.shape,
        atm_state,
        flux_here,
        surface_to_atm,
        atm_gain[:1],
        scratch=[pltpu.VMEM(atm_state.shape, jnp.bfloat16), pltpu.SemaphoreType.DMA((3,))],
        away=True,
        room=24000000,
    )
    rings = lax.all_to_all(
        normed.reshape(lon_count, lats, lon_dev, width), LON, 0, 0, tiled=True
    )
    flux_sea = together(kept_atm, lax.ppermute(sent_atm, "comp", swap), 1)
    ocean_in = (
        ocean_state.astype(jnp.float32)
        + wet * jnp.dot(flux_sea, surface_to_ocean, preferred_element_type=jnp.float32)
    ).astype(jnp.bfloat16)
    west = shifted(ocean_in[:, -HALO:], 0, 1)
    east = shifted(ocean_in[:, :HALO], 0, -1)
    upper, lower = [
        jnp.concatenate([west[part], ocean_in[part], east[part]], axis=1)
        for part in (slice(0, REACH), slice(REACH, None))
    ]
    seen = (order[:, None] * lats + np.arange(lats)).reshape(-1)
    moved = jnp.asarray(np.eye(lat_total)[:, seen].astype(ml_dtypes.bfloat16))
    weight = quad_weight.reshape(lax.axis_size("y"), -1, lats).swapaxes(0, 1).reshape(1, -1)
    weighted, turned, mix = prepare(legendre, moved, weight / lat_total, spec_real, spec_imag)
    gain_row = degree_gain[None]
    rings, upper, lower, weighted, turned, mix, gain_row = lax.optimization_barrier(
        (rings, upper, lower, weighted, turned, mix, gain_row)
    )
    spectrum = waves(
        (owners, lats, owned, width), forward, rings, lax.ppermute(rings, "comp", swap)
    )
    spectrum, upper, lower = lax.optimization_barrier((spectrum, upper, lower))
    gathered = lax.all_to_all(spectrum, OWNERS, 0, 0, tiled=True)
    first_col = lax.axis_index(LON) * sea_cols
    kernels = jnp.broadcast_to(
        ocean_kernel.astype(jnp.float32).reshape(2, STENCIL_TAPS**2, 1, sea_width),
        (2, STENCIL_TAPS**2, 8, sea_width),
    )
    ocean = (kernels, ocean_gain, ocean_up, ocean_down)
    north, south = shifted(lower, 1, 0), shifted(upper, -1, 0)
    filtered = call(
        filter_kernel,
        (lat_total, owned, width),
        gain_row,
        gathered.reshape(lat_total, owned, width),
        weighted,
        mix,
        turned,
        scratch=[
            pltpu.VMEM((lat_total, owned, width), jnp.bfloat16),
            pltpu.VMEM(weighted.shape, jnp.bfloat16),
            pltpu.VMEM((2 * width, 2 * width), jnp.bfloat16),
            pltpu.VMEM(turned.shape, jnp.bfloat16),
            pltpu.VMEM((owned // 2, lat_total, 2 * width), jnp.bfloat16),
            pltpu.VMEM((lat_total, owned, width), jnp.bfloat16),
            pltpu.SemaphoreType.DMA((3 + lat_total // 64 * 2,)),
        ],
        behind=4,
        away=True,
        room=100_000,
    )
    filtered, *pieces = lax.optimization_barrier((filtered, north, upper, lower, south))
    returned = lax.all_to_all(
        filtered.reshape(owners, lats, owned, width), OWNERS, 0, 0, tiled=True
    )
    upper, lower = ocean_block(first_col - LEAD, circle, pieces, *ocean, 0, 2)
    north, south = shifted(lower, 1, 0), shifted(upper, -1, 0)
    returned, *pieces = lax.optimization_barrier((returned, north, upper, lower, south))
    spatial = waves(
        (lon_count, lats, lon_dev, width), inverse, returned, lax.ppermute(returned, "comp", swap)
    )
    spatial, *pieces = lax.optimization_barrier((spatial, *pieces))
    spectral = lax.all_to_all(spatial, LON, 0, 0, tiled=True).reshape(lat_dev, lon_dev, width)
    (current,) = ocean_block(first_col, circle, pieces, *ocean, 1, 1)
    ocean_out = jnp.where(wet_mask[:, :, None] == 1, current, ocean_state)
    spectral, ocean_out = lax.optimization_barrier((spectral, ocean_out))
    atm_out = epilogue(
        atm_state, flux_here, spectral, surface_to_atm, atm_gain[1:], atm_up, atm_down
    )
    return (atm_out, ocean_out)


def solution(mesh):
    lat_count, lon_count = mesh.shape["lat"], mesh.shape["lon"]
    torus = Mesh(
        mesh.devices.reshape(4, lat_count // 4, lon_count // 4, 4, mesh.shape["comp"]), ALL
    )
    atm, sea = P(LAT, (*LON, "comp"), None), P((*LAT, "comp"), LON, None)
    placed = (atm, sea, P((*LAT, "comp"), LON), P(ALL, None, None)) + (P(),) * 15
    return jax.shard_map(
        local, mesh=torus, in_specs=placed, out_specs=(atm, sea), check_vma=False
    )
```

```python
import math

import jax
import jax.numpy as jnp
import ml_dtypes
import numpy as np
from jax import lax
from jax.experimental import pallas as pl
from jax.experimental.pallas import tpu as pltpu
from jax.sharding import Mesh
from jax.sharding import PartitionSpec as P

MODES = 512
STENCIL_TAPS = 7
OCEAN_DILATION = 2
LAT = ("y", "z_hi")
LON = ("z_lo", "x")
ALL = (*LAT, *LON, "comp")
OWNERS = ("z_hi", "z_lo", "x", "y")


epsilon = 1e-05


def owner_order():
    count = lax.axis_size(LAT) * lax.axis_size(LON)
    return np.arange(count).reshape(lax.axis_size("y"), -1).T.reshape(-1)


def wave_tables(owners, lon_count, circle, owned):
    rows = (owners[:, None] * owned + np.arange(owned)).reshape(-1)
    block = circle // (2 * lon_count)
    where = np.arange(lon_count * block)
    forward, inverse = [], []
    row_sets = [rows // owned * 2 * owned + q * owned + rows % owned for q in range(2)]
    place_sets = [(where // block * 2 + q) * block + where % block for q in range(2)]

    def waves(row, place):
        phase = (row[:, None] // 2) * place[None, :] % circle
        angle = phase.astype(np.float32) * np.float32(2.0 * math.pi / circle)
        return np.where((row % 2 == 0)[:, None], np.cos(angle), -np.sin(angle)).astype(np.float32)

    for own in range(2):
        order = (own, 1 - own)
        f = np.concatenate([waves(row_sets[own], place_sets[q]) for q in order], 1)
        forward.append(f / np.float32(math.sqrt(circle)))
        g = []
        for q in order:
            factor = np.where(row_sets[q] // 2 == 0, 1.0, 2.0).astype(np.float32)
            g.append((waves(row_sets[q], place_sets[own]) * factor[:, None]).T)
        inverse.append(np.concatenate(g, 1) / np.float32(math.sqrt(circle)))
    return (
        np.stack(forward).astype(ml_dtypes.bfloat16),
        np.stack(inverse).astype(ml_dtypes.bfloat16),
    )


def waves_kernel(
    table_hbm, own_hbm, other_hbm, out_hbm, table_ref, own_ref, other_ref, held, sems
):
    lats, width = own_ref.shape[0], own_ref.shape[3]
    half = table_ref.shape[1] // 2
    table = pltpu.make_async_copy(table_hbm, table_ref, sems.at[0])
    table.start()
    owns, others, sends = [], [], []
    for i in range(lats):
        owns.append(pltpu.make_async_copy(own_hbm.at[:, i], own_ref.at[i], sems.at[1 + i]))
        owns[-1].start()
        at = sems.at[1 + lats + i]
        others.append(pltpu.make_async_copy(other_hbm.at[:, i], other_ref.at[i], at))
        others[-1].start()
    table.wait()
    for i in range(lats):
        owns[i].wait()
        total = jnp.dot(
            table_ref[:, :half],
            own_ref[i].reshape(half, width),
            preferred_element_type=jnp.float32,
        )
        others[i].wait()
        total += jnp.dot(
            table_ref[:, half:],
            other_ref[i].reshape(half, width),
            preferred_element_type=jnp.float32,
        )
        held[i] = total.astype(jnp.bfloat16).reshape(held.shape[1:])
        at = sems.at[1 + 2 * lats + i]
        sends.append(pltpu.make_async_copy(held.at[i], out_hbm.at[:, i], at))
        sends[-1].start()
    for send in sends:
        send.wait()


def waves(shape, table, own, other):
    lats = shape[1]
    return call(
        waves_kernel,
        shape,
        table,
        own,
        other,
        scratch=[
            pltpu.VMEM(table.shape, jnp.bfloat16),
            pltpu.VMEM((lats, own.shape[0], *own.shape[2:]), jnp.bfloat16),
            pltpu.VMEM((lats, own.shape[0], *own.shape[2:]), jnp.bfloat16),
            pltpu.VMEM((lats, shape[0], *shape[2:]), jnp.bfloat16),
            pltpu.SemaphoreType.DMA((1 + 3 * lats,)),
        ],
        behind=3,
        away=True,
    )


def filter_kernel(
    gain_ref,
    spectrum_hbm,
    weights_hbm,
    out_hbm,
    spectrum_ref,
    weighted_ref,
    mix_ref,
    turned_ref,
    rows_ref,
    held,
    sems,
):
    count = weighted_ref.shape[0]
    lats, owned, width = spectrum_ref.shape
    block = 64
    side = block * owned
    parts = lats // block
    targets = [weighted_ref.at[m] for m in range(count)]
    targets += [mix_ref.at[:, h * width : (h + 1) * width] for h in range(2)]
    targets += [turned_ref.at[m] for m in range(count)]
    arrivals = []
    for b in range(parts):
        part = pl.ds(b * block, block)
        at = sems.at[len(targets) + b]
        arrivals.append(pltpu.make_async_copy(spectrum_hbm.at[part], spectrum_ref.at[part], at))
        arrivals[-1].start()
    fetches, at = [], 0
    for n, target in enumerate(targets):
        size = target.shape[0]
        fetches.append(
            pltpu.make_async_copy(weights_hbm.at[pl.ds(at, size)], target, sems.at[n])
        )
        fetches[-1].start()
        at += size
    r = lax.broadcasted_iota(jnp.int32, (side, side), 0)
    s = lax.broadcasted_iota(jnp.int32, (side, side), 1)
    pick = jnp.where((r % block) * owned + r // block == s, 1.0, 0.0).astype(jnp.bfloat16)
    back = jnp.where((s % block) * owned + s // block == r, 1.0, 0.0).astype(jnp.bfloat16)

    def columns(p):
        return slice(p % 2 * width, (p % 2 + 1) * width)

    for b in range(parts):
        span = slice(b * block, (b + 1) * block)
        arrivals[b].wait()
        piece = spectrum_ref[span].reshape(side, width)
        moved = jnp.dot(pick, piece, preferred_element_type=jnp.float32).astype(jnp.bfloat16)
        for p in range(owned):
            rows_ref[p // 2, span, columns(p)] = moved[p * block : (p + 1) * block]
    gain = jnp.transpose(jnp.broadcast_to(gain_ref[...], (8, lats)))[:, :1]
    for fetch in fetches:
        fetch.wait()
    for m in range(count):
        coeffs = jnp.dot(weighted_ref[m], rows_ref[m], preferred_element_type=jnp.float32)
        mixed = jnp.dot(
            coeffs.astype(jnp.bfloat16), mix_ref[...], preferred_element_type=jnp.float32
        )
        filtered = (mixed * gain).astype(jnp.bfloat16)
        rows_ref[m] = jnp.dot(
            turned_ref[m], filtered, preferred_element_type=jnp.float32
        ).astype(jnp.bfloat16)
    sends = []
    for b in range(parts):
        span = slice(b * block, (b + 1) * block)
        piece = jnp.concatenate(
            [rows_ref[p // 2, span, columns(p)] for p in range(owned)], axis=0
        )
        moved = jnp.dot(back, piece, preferred_element_type=jnp.float32).astype(jnp.bfloat16)
        held[span] = moved.reshape(block, owned, width)
        at = sems.at[len(targets) + parts + b]
        part = pl.ds(b * block, block)
        sends.append(pltpu.make_async_copy(held.at[part], out_hbm.at[part], at))
        sends[-1].start()
    for send in sends:
        send.wait()


VMEM = 62_900_000


def call(kernel, shape, *args, scratch=(), room=0, scalars=0, behind=0, away=False):
    spaces = [pltpu.SMEM] * scalars + [pltpu.VMEM] * (len(args) - scalars - behind)
    spaces += [pltpu.HBM] * behind
    return pl.pallas_call(
        kernel,
        out_shape=jax.ShapeDtypeStruct(shape, jnp.bfloat16),
        in_specs=[pl.BlockSpec(memory_space=space) for space in spaces],
        out_specs=pl.BlockSpec(memory_space=pltpu.HBM if away else pltpu.VMEM),
        scratch_shapes=list(scratch),
        compiler_params=pltpu.CompilerParams(vmem_limit_bytes=VMEM - room),
    )(*args)


def gelu(x):
    inner = x * (math.sqrt(2.0 / math.pi) + (math.sqrt(2.0 / math.pi) * 0.044715) * (x * x))
    half = 0.5 * x
    return half + half * jnp.tanh(inner)


def normalised(values, gain):
    centred = values - jnp.mean(values, axis=-1, keepdims=True)
    spread = jnp.mean(centred * centred, axis=-1, keepdims=True)
    return (centred * lax.rsqrt(spread + epsilon) * gain).astype(jnp.bfloat16)


def prologue_kernel(atm_ref, flux_ref, out_weight_ref, gain_ref, out_hbm, held, sems):
    rows, lon_dev, width = atm_ref.shape
    each = rows // sems.shape[0]
    sends = []
    for k in range(sems.shape[0]):
        part = pl.ds(k * each, each)
        flux = flux_ref[pl.ds(k * each * lon_dev, each * lon_dev)]
        forced = atm_ref[part].reshape(each * lon_dev, width).astype(jnp.float32) + jnp.dot(
            flux, out_weight_ref[...], preferred_element_type=jnp.float32
        )
        held[part] = normalised(forced, gain_ref[...]).reshape(each, lon_dev, width)
        sends.append(pltpu.make_async_copy(held.at[part], out_hbm.at[part], sems.at[k]))
        sends[-1].start()
    for send in sends:
        send.wait()


def epilogue_kernel(
    atm_ref, flux_ref, spectral_ref, out_weight_ref, gain_ref, up_ref, down_ref, out_ref
):
    rows, lon_dev, width = atm_ref.shape
    each = rows // 2
    side = each * lon_dev
    for k in range(2):
        part = pl.ds(k * each, each)
        forced = atm_ref[part].reshape(side, width).astype(jnp.float32) + jnp.dot(
            flux_ref[pl.ds(k * side, side)],
            out_weight_ref[...],
            preferred_element_type=jnp.float32,
        )
        mixed = forced + spectral_ref[part].reshape(side, width).astype(jnp.float32)
        normed = normalised(mixed, gain_ref[...])
        hidden = gelu(jnp.dot(normed, up_ref[...], preferred_element_type=jnp.float32))
        total = mixed + jnp.dot(
            hidden.astype(jnp.bfloat16), down_ref[...], preferred_element_type=jnp.float32
        )
        out_ref[part] = total.astype(jnp.bfloat16).reshape(each, lon_dev, width)


def epilogue(atm, flux, spectral, *weights, rows=8):
    lat_dev, lon_dev, width = atm.shape
    field = pl.BlockSpec((rows, lon_dev, width), lambda i: (i, 0, 0))
    specs = [field, pl.BlockSpec((rows * lon_dev, flux.shape[1]), lambda i: (i, 0)), field]
    specs += [pl.BlockSpec(w.shape, lambda i: (0, 0)) for w in weights]
    return pl.pallas_call(
        epilogue_kernel,
        grid=(lat_dev // rows,),
        out_shape=jax.ShapeDtypeStruct(atm.shape, jnp.bfloat16),
        in_specs=specs,
        out_specs=field,
        compiler_params=pltpu.CompilerParams(vmem_limit_bytes=VMEM - 38000000),
    )(atm, flux, spectral, *weights)


HALO = 16
LEAD = 8
LANES = 128
REACH = STENCIL_TAPS // 2 * OCEAN_DILATION


def ocean_rows(field, kern, gain, up, down, sums, out_ref, group, bounds):
    blocks = field.shape[0]
    rows, cols, width = out_ref.shape
    stride = cols // 8
    each = stride // OCEAN_DILATION

    def step(g, carry):
        top = g * group
        for r in range(group):
            for lane in range(blocks):
                part = slice(lane * LANES, (lane + 1) * LANES)
                for parity in range(OCEAN_DILATION):
                    acc = [None] * each
                    for a in range(STENCIL_TAPS):
                        row = top + r + a * OCEAN_DILATION
                        first = LEAD - REACH + parity
                        loads = [
                            field[lane, row, pl.ds(first + OCEAN_DILATION * q, 8, stride=stride), :]
                            for q in range(each + STENCIL_TAPS - 1)
                        ]
                        for b in range(STENCIL_TAPS):
                            weight = kern[a * STENCIL_TAPS + b, :, part]
                            for q in range(each):
                                term = loads[q + b] * weight
                                acc[q] = term if acc[q] is None else acc[q] + term
                    for q in range(each):
                        at = pl.ds(parity + OCEAN_DILATION * q, 8, stride=stride)
                        sums[lane, r, at, :] = acc[q]
        side = group * cols
        stencil = jnp.concatenate(
            [sums[lane].reshape(side, LANES) for lane in range(blocks)], axis=1
        )
        normed = normalised(stencil, gain[...])
        hidden = gelu(jnp.dot(normed, up[...], preferred_element_type=jnp.float32))
        total = jnp.dot(
            hidden.astype(jnp.bfloat16), down[...], preferred_element_type=jnp.float32
        )
        for r in range(group):
            centre = jnp.concatenate(
                [field[lane, top + r + REACH, LEAD : LEAD + cols, :] for lane in range(blocks)],
                axis=1,
            )
            value = centre + total[r * cols : (r + 1) * cols]
            row_low, row_high, low, high = bounds
            high = jnp.where((top + r >= row_low) & (top + r < row_high), high, low)
            col = lax.broadcasted_iota(jnp.int32, value.shape, 0)
            value = jnp.where((col >= low) & (col < high), value, 0.0)
            out_ref[top + r] = value.astype(jnp.bfloat16)
        return carry

    lax.fori_loop(0, rows // group, step, 0)


def ocean_kernel(inside_ref, *refs):
    *pieces, kern_ref, gain_ref, up_ref, down_ref, out_ref, field, sums = refs
    at = 0
    for ref in pieces:
        for lane in range(field.shape[0]):
            field[lane, at : at + ref.shape[0]] = ref[
                :, :, lane * LANES : (lane + 1) * LANES
            ].astype(jnp.float32)
        at += ref.shape[0]
    bounds = [inside_ref[n] for n in range(4)]
    ocean_rows(
        field, kern_ref, gain_ref, up_ref, down_ref, sums, out_ref, sums.shape[1], bounds
    )


def ocean_block(corner, extent, pieces, kern, gain, up, down):
    rows = sum(piece.shape[0] for piece in pieces)
    cols, width = pieces[0].shape[1:]
    blocks, out_rows, out_cols = width // LANES, rows - 2 * REACH, cols - 2 * LEAD
    bounds = [side for at, size in zip(corner, extent) for side in (-at, size - at)]
    return call(
        ocean_kernel,
        (out_rows, out_cols, width),
        jnp.stack(bounds).astype(jnp.int32),
        *pieces,
        kern,
        gain,
        up,
        down,
        scratch=[
            pltpu.VMEM((blocks, rows, cols, LANES), jnp.float32),
            pltpu.VMEM((blocks, 4, out_cols, LANES), jnp.float32),
        ],
        scalars=1,
        room=38_000_000,
    )


def shifted(block, dy, dx):
    tall = lax.axis_size(LAT) * lax.axis_size("comp")
    broad = lax.axis_size(LON)

    def place(y, x):
        return (y // 2 * broad + x) * 2 + y % 2

    pairs = [
        (place(y, x), place(y + dy, x + dx))
        for y in range(tall)
        for x in range(broad)
        if 0 <= y + dy < tall and 0 <= x + dx < broad
    ]
    return lax.ppermute(block, ALL, pairs)


def local(
    atm_state,
    ocean_state,
    wet_mask,
    legendre,
    quad_weight,
    spec_real,
    spec_imag,
    degree_gain,
    atm_gain,
    atm_up,
    atm_down,
    atm_to_surface,
    surface_to_atm,
    ocean_to_surface,
    surface_to_ocean,
    ocean_kernel,
    ocean_gain,
    ocean_up,
    ocean_down,
):
    lat_count = lax.axis_size(LAT)
    lon_count = lax.axis_size(LON)
    lat_dev, lon_dev, width = atm_state.shape
    sea_rows, sea_cols, sea_width = ocean_state.shape
    lat_total = lat_dev * lat_count
    circle = lon_dev * lon_count * 2
    owned = 2 * legendre.shape[0]
    owners = lat_count * lon_count
    order = owner_order()
    lats = lat_dev // lon_count
    me = lax.axis_index("comp")
    swap = [(0, 1), (1, 0)]
    forward, inverse = wave_tables(order, lon_count, circle, owned)
    forward = lax.dynamic_index_in_dim(jnp.asarray(forward), me, 0, keepdims=False)
    inverse = lax.dynamic_index_in_dim(jnp.asarray(inverse), me, 0, keepdims=False)
    wet = wet_mask.astype(jnp.float32)[:, :, None]
    ocean_flux = (
        jnp.dot(ocean_state, ocean_to_surface, preferred_element_type=jnp.float32) * wet
    ).astype(jnp.bfloat16)
    atm_flux = jnp.dot(atm_state, atm_to_surface, preferred_element_type=jnp.float32).astype(
        jnp.bfloat16
    )

    def halves(mine, dim):
        low, high = jnp.split(mine, 2, axis=dim)
        return (jnp.where(me == 0, low, high), jnp.where(me == 0, high, low))

    def together(kept, got, dim):
        low = jnp.where(me == 0, kept, got)
        high = jnp.where(me == 0, got, kept)
        return jnp.concatenate([low, high], axis=dim)

    kept_ocean, sent_ocean = halves(ocean_flux, 1)
    kept_atm, sent_atm = halves(atm_flux, 0)
    got_ocean = lax.ppermute(sent_ocean, "comp", swap)
    flux_here = together(kept_ocean, got_ocean, 0).reshape(lat_dev * lon_dev, -1)
    normed = call(
        prologue_kernel,
        atm_state.shape,
        atm_state,
        flux_here,
        surface_to_atm,
        atm_gain[:1],
        scratch=[pltpu.VMEM(atm_state.shape, jnp.bfloat16), pltpu.SemaphoreType.DMA((3,))],
        away=True,
        room=24000000,
    )
    rings = lax.all_to_all(
        normed.reshape(lon_count, lats, lon_dev, width), LON, 0, 0, tiled=True
    )
    flux_sea = together(kept_atm, lax.ppermute(sent_atm, "comp", swap), 1)
    ocean_in = (
        ocean_state.astype(jnp.float32)
        + wet * jnp.dot(flux_sea, surface_to_ocean, preferred_element_type=jnp.float32)
    ).astype(jnp.bfloat16)
    west = shifted(ocean_in[:, -HALO:], 0, 1)
    east = shifted(ocean_in[:, :HALO], 0, -1)
    broad = jnp.concatenate([west, ocean_in, east], axis=1)
    rings, broad = lax.optimization_barrier((rings, broad))
    seen = (order[:, None] * lats + np.arange(lats)).reshape(-1)
    moved = jnp.asarray(np.eye(lat_total)[:, seen].astype(ml_dtypes.bfloat16))
    table = jnp.einsum(
        "mlt,ts->mls", legendre, moved, preferred_element_type=jnp.float32
    ).astype(jnp.bfloat16)
    weight = quad_weight.reshape(lax.axis_size("y"), -1, lats).swapaxes(0, 1).reshape(-1)
    weighted = (table.astype(jnp.float32) * (weight / lat_total)).astype(jnp.bfloat16)
    turned = jnp.swapaxes(table, 1, 2)
    spectrum = waves(
        (owners, lats, owned, width), forward, rings, lax.ppermute(rings, "comp", swap)
    )
    spectrum, broad = lax.optimization_barrier((spectrum, broad))
    gathered = lax.all_to_all(spectrum, OWNERS, 0, 0, tiled=True)
    north, south = shifted(broad, 1, 0), shifted(broad, -1, 0)
    weights = jnp.concatenate(
        [*weighted, spec_real, -spec_imag, spec_imag, spec_real, *turned], axis=0
    )
    filtered = call(
        filter_kernel,
        (lat_total, owned, width),
        degree_gain[None],
        gathered.reshape(lat_total, owned, width),
        weights,
        scratch=[
            pltpu.VMEM((lat_total, owned, width), jnp.bfloat16),
            pltpu.VMEM(weighted.shape, jnp.bfloat16),
            pltpu.VMEM((2 * width, 2 * width), jnp.bfloat16),
            pltpu.VMEM(turned.shape, jnp.bfloat16),
            pltpu.VMEM((owned // 2, lat_total, 2 * width), jnp.bfloat16),
            pltpu.VMEM((lat_total, owned, width), jnp.bfloat16),
            pltpu.SemaphoreType.DMA((6 + lat_total // 64 * 2,)),
        ],
        behind=2,
        away=True,
        room=100000,
    )
    filtered, broad, north, south = lax.optimization_barrier((filtered, broad, north, south))
    returned = lax.all_to_all(
        filtered.reshape(owners, lats, owned, width), OWNERS, 0, 0, tiled=True
    )
    first_row = lax.axis_index((*LAT, "comp")) * sea_rows
    first_col = lax.axis_index(LON) * sea_cols
    extent = (lat_total, circle)
    kernels = jnp.broadcast_to(
        ocean_kernel.astype(jnp.float32).reshape(2, STENCIL_TAPS**2, 1, sea_width),
        (2, STENCIL_TAPS**2, 8, sea_width),
    )
    blocks = [
        (kernels[k], ocean_gain[k : k + 1], ocean_up[k], ocean_down[k]) for k in range(2)
    ]
    corner = (first_row - REACH, first_col - LEAD)
    first = ocean_block(corner, extent, (north, broad, south), *blocks[0])
    returned, first = lax.optimization_barrier((returned, first))
    spatial = waves(
        (lon_count, lats, lon_dev, width), inverse, returned, lax.ppermute(returned, "comp", swap)
    )
    spatial, first = lax.optimization_barrier((spatial, first))
    spectral = lax.all_to_all(spatial, LON, 0, 0, tiled=True).reshape(lat_dev, lon_dev, width)
    current = ocean_block((first_row, first_col), extent, (first,), *blocks[1])
    ocean_out = jnp.where(wet_mask[:, :, None] == 1, current, ocean_state)
    spectral, ocean_out = lax.optimization_barrier((spectral, ocean_out))
    atm_out = epilogue(
        atm_state, flux_here, spectral, surface_to_atm, atm_gain[1:], atm_up, atm_down
    )
    return (atm_out, ocean_out)


def solution(mesh):
    lat_count, lon_count = mesh.shape["lat"], mesh.shape["lon"]
    torus = Mesh(
        mesh.devices.reshape(4, lat_count // 4, lon_count // 4, 4, mesh.shape["comp"]), ALL
    )
    atm, sea = P(LAT, (*LON, "comp"), None), P((*LAT, "comp"), LON, None)
    placed = (atm, sea, P((*LAT, "comp"), LON), P(ALL, None, None)) + (P(),) * 15
    return jax.shard_map(
        local, mesh=torus, in_specs=placed, out_specs=(atm, sea), check_vma=False
    )
```
